256 devices in a mesh: tensor: 8 (over z), expert: 32 (over y, x, core).
Axes of the slice: x: 4, y: 4, z: 8, core: 2. Of those that a mesh axis runs over, the one named last changes fastest.
Arguments:
- tokens: bfloat16 [4096, 7168], P('expert', 'tensor'), may hold values from -6 to 6
- route_ids: int32 [4096, 2], P('expert'), may hold values from 0 to 31, all different within a row; in each aligned block of 128 rows (0 to 127, 128 to 255, ...) at most 16 rows name the same one
- route_weights: float32 [4096, 2], P('expert'), may hold values from 0.1 to 1
- cotangent: bfloat16 [4096, 7168], P('expert', 'tensor'), may hold values from -6 to 6
- w_gate: bfloat16 [32, 7168, 1024], P('expert', None, 'tensor'), may hold values from -0.0625 to 0.0625
- w_up: bfloat16 [32, 7168, 1024], P('expert', None, 'tensor'), may hold values from -0.0625 to 0.0625
- w_down: bfloat16 [32, 1024, 7168], P('expert', 'tensor'), may hold values from -0.1875 to 0.1875
Outputs:
- mixed: bfloat16 [4096, 7168], P('expert', 'tensor')
- grad_tokens: bfloat16 [4096, 7168], P('expert', 'tensor')
- grad_route: float32 [4096, 2], P('expert')
- grad_gate: bfloat16 [32, 7168, 1024], P('expert', None, 'tensor')
- grad_up: bfloat16 [32, 7168, 1024], P('expert', None, 'tensor')
- grad_down: bfloat16 [32, 1024, 7168], P('expert', 'tensor')
The draws below stay inside these ranges and needn't reach their ends.
Inputs may be any that keep to these rules, and one draw needn't show every extreme that they name: `route_ids`: each row names 2 different experts. In each aligned block of 128 rows (the rows of one device) no expert is named by more than 16 rows, and in some block one expert is named by exactly 16 rows.
All inputs are finite; a program needn't handle non-finite values.
Results may differ from the reference program's by a relative error of at most 0.015.
Values may be sent and summed in bfloat16 or wider, within the bound.
A program may use at most 128 MiB of HBM per device.

```python
import math
import jax
import jax.numpy as jnp
import numpy as np
from jax import lax

D = 7168
FF = 1024
TOPK = 2
TOK_DEV = 128
EXPERTS = 32
CAP = 16
TOKENS = 4096
N_TENSOR = 8
N_EXPERT = 32


def levels(stream_key, dims, cuts, low, top_value):
    loudness, own = 1.0, jax.random.fold_in(stream_key, 6)
    for dim, blocks in cuts:
        steps = jnp.exp(jax.random.uniform(jax.random.fold_in(own, dim), (blocks,), jnp.float32, low / len(cuts), top_value / len(cuts)))
        loudness = loudness * jnp.repeat(steps, dims[dim] // blocks).reshape([-1 if axis == dim else 1 for axis in range(len(dims))])
    return loudness


def deal_out(own_key, own, number, rows, number_of, top, bound, skew):
    order = jax.random.permutation(own_key, number_of)
    heavy_load, usual = portions_of(number_of, rows * top, bound, skew, True), portions_of(number_of, rows * top, bound, skew, False)
    places = jnp.arange(number_of)

    def named(lengths, rotation):
        used = int((lengths > 0).sum())
        fixed = max(1, used // 4)
        passed = fixed + (places - fixed + rotation * (used - fixed)) % max(1, number_of - fixed)
        return jnp.zeros((number_of,), jnp.int32).at[order[jnp.where(places < fixed, places, passed)]].set(jnp.asarray(lengths, jnp.int32))

    lengths = jnp.where(number % 4 == 0, named(heavy_load, number // 4), named(usual, number - number // 4 - 1))
    mixed = jax.random.permutation(jax.random.fold_in(own, 3), number_of)
    source_of, receiver = mixed[0:number_of // 2 * 2:2], mixed[1:number_of // 2 * 2:2]
    slack = jnp.minimum(lengths[source_of] - 1, bound - lengths[receiver]) // 2
    slack = jnp.where((source_of == order[0]) | (receiver == order[0]) | (lengths[receiver] == 0), 0, jnp.maximum(slack, 0))
    passed = jax.random.randint(jax.random.fold_in(own, 4), (number_of // 2,), 0, 1 << 20) % (slack + 1)
    lengths = lengths.at[source_of].add(-passed).at[receiver].add(passed)
    items = jnp.searchsorted(jnp.cumsum(lengths), jnp.arange(rows * top), side="right").astype(jnp.int32)
    grid = items.reshape(top, rows).T
    grid = grid[jax.random.permutation(jax.random.fold_in(own, 1), rows)]
    rotation = jax.random.randint(jax.random.fold_in(own, 2), (rows, 1), 0, top)
    return jnp.take_along_axis(grid, (jnp.arange(top)[None, :] + rotation) % top, axis=1)


def portions_of(number_of, total, reach, skew, full):
    loads = [(1 << 20) // math.isqrt(standing ** skew) + 1 for standing in range(1, number_of + 1)]
    largest = reach if full else min(reach, max(-(-total // number_of), total * loads[0] // sum(loads)))
    least = 1 if total - largest >= number_of - 1 else 0
    holding, surplus = [largest] + [least] * (number_of - 1), total - largest - least * (number_of - 1)
    while surplus > 0:
        movable = [i for i in range(1, number_of) if holding[i] < largest] or [i for i in range(1, number_of) if holding[i] < reach]
        whole, remaining = sum([loads[i] for i in movable]), surplus
        for i in movable:
            extra = min(reach - holding[i], max(1, remaining * loads[i] // whole), surplus)
            holding[i] = holding[i] + extra
            surplus = surplus - extra
    return np.array(holding)


def bell_draw(own_key, extent, width, reach, cuts=(), kind=jnp.bfloat16):
    loudness = levels(own_key, extent, cuts, -0.22, 0.18) if cuts else 1.0
    result = jax.random.normal(own_key, extent, jnp.float32) * width * loudness
    return jnp.minimum(jnp.maximum(result, -reach), reach).astype(kind)


def setup_inputs(seed: int = 0) -> dict:
    key_list = jax.random.split(jax.random.key(seed), 8)
    tokens = bell_draw(key_list[0], (TOKENS, D), 1.0, 6.0, ((0, 32), (1, 8)))
    route_ids_keys = jax.random.split(jax.random.fold_in(key_list[1], 1), TOKENS // TOK_DEV)
    route_ids_turns = jax.random.permutation(jax.random.fold_in(key_list[1], 3), TOKENS // TOK_DEV)
    route_ids = jax.vmap(lambda own, number: deal_out(jax.random.fold_in(key_list[1], 2), own, number, TOK_DEV, EXPERTS, TOPK, CAP, 2))(route_ids_keys, route_ids_turns).reshape((TOKENS, TOPK))
    route_weights = jnp.clip(jnp.exp(math.log(1.0) - 2.3025851 * jax.random.uniform(key_list[2], (TOKENS, TOPK), jnp.float32) ** levels(key_list[2], (TOKENS, TOPK), ((0, 32),), -0.2, 0.2)), 0.1, 1.0)
    cotangent = bell_draw(key_list[3], (TOKENS, D), 1.0, 6.0, ((0, 32), (1, 8)))
    w_gate = bell_draw(key_list[4], (EXPERTS, D, FF), D ** -0.5, 0.0625, ((0, 32), (2, 8)))
    w_up = bell_draw(key_list[5], (EXPERTS, D, FF), D ** -0.5, 0.0625, ((0, 32), (2, 8)))
    w_down = bell_draw(key_list[6], (EXPERTS, FF, D), FF ** -0.5, 0.1875, ((0, 32), (1, 8)))
    return {"tokens": tokens, "route_ids": route_ids, "route_weights": route_weights, "cotangent": cotangent, "w_gate": w_gate, "w_up": w_up, "w_down": w_down}


def slot_positions(route_ids):
    flat_ids = route_ids.reshape(N_EXPERT, TOK_DEV * TOPK)
    labels = jnp.arange(EXPERTS, dtype=jnp.int32)
    onehot = (flat_ids[:, :, None] == labels[None, None, :]).astype(jnp.int32)
    before = jnp.cumsum(onehot, axis=1) - onehot
    slot_index = jnp.sum(before * onehot, axis=2)
    source_block = jnp.arange(N_EXPERT, dtype=jnp.int32)[:, None]
    target = (flat_ids * N_EXPERT + source_block) * CAP + slot_index
    return target.reshape(TOKENS * TOPK).astype(jnp.int32)


def per_block_total(parts):
    rounded = lax.optimization_barrier(parts.astype(jnp.bfloat16))
    return jnp.sum(rounded.astype(jnp.float32), axis=0)


def column_split(matrix):
    block_width = FF // N_TENSOR
    return matrix.astype(jnp.float32).reshape(matrix.shape[0], N_TENSOR, block_width).transpose(1, 0, 2)


def expert_pass(operands):
    rows, cot_rows, gate_matrix, up_matrix, down_weight = operands
    block_width = FF // N_TENSOR
    row_pairs = (((1,), (1,)), ((), ()))
    col_pairs = (((0,), (0,)), ((), ()))
    gate_proj = jnp.dot(rows, gate_matrix, preferred_element_type=jnp.float32)
    up_proj = jnp.dot(rows, up_matrix, preferred_element_type=jnp.float32)
    hidden_state = (jax.nn.silu(gate_proj) * up_proj).astype(jnp.bfloat16)
    down_block_list = down_weight.astype(jnp.float32).reshape(N_TENSOR, block_width, D)
    expert_output = per_block_total(jnp.einsum("zej,zjq->zeq", column_split(hidden_state), down_block_list)).astype(jnp.bfloat16)
    d_hidden = lax.dot_general(cot_rows, down_weight, row_pairs, preferred_element_type=jnp.float32)
    grad_down = lax.dot_general(hidden_state, cot_rows, col_pairs, preferred_element_type=jnp.float32).astype(jnp.bfloat16)
    sigmoid_gate = jax.nn.sigmoid(gate_proj)
    gate_gradient = (d_hidden * up_proj * sigmoid_gate * (1.0 + gate_proj * (1.0 - sigmoid_gate))).astype(jnp.bfloat16)
    up_gradient = (d_hidden * jax.nn.silu(gate_proj)).astype(jnp.bfloat16)
    grad_gate = lax.dot_general(rows, gate_gradient, col_pairs, preferred_element_type=jnp.float32).astype(jnp.bfloat16)
    grad_up = lax.dot_general(rows, up_gradient, col_pairs, preferred_element_type=jnp.float32).astype(jnp.bfloat16)
    backward_pieces = jnp.einsum("snu,syu->sny", column_split(gate_gradient), column_split(gate_matrix))
    backward_pieces = backward_pieces + jnp.einsum("snu,syu->sny", column_split(up_gradient), column_split(up_matrix))
    input_rows = per_block_total(backward_pieces).astype(jnp.bfloat16)
    return expert_output, input_rows, grad_gate, grad_up, grad_down


def reference(tokens, route_ids, route_weights, cotangent, w_gate, w_up, w_down):
    target = slot_positions(route_ids)
    pair_rows = jnp.repeat(tokens, TOPK, axis=0)
    weight_flat = route_weights.reshape(TOKENS * TOPK)
    cot_pairs = (weight_flat[:, None] * jnp.repeat(cotangent, TOPK, axis=0).astype(jnp.float32)).astype(jnp.bfloat16)
    buffer_rows = EXPERTS * N_EXPERT * CAP
    routed = jnp.zeros((buffer_rows, D), jnp.bfloat16).at[target].set(pair_rows)
    routed_cot = jnp.zeros((buffer_rows, D), jnp.bfloat16).at[target].set(cot_pairs)
    stacked_shape = (EXPERTS, N_EXPERT * CAP, D)
    expert_output, input_rows, grad_gate, grad_up, grad_down = lax.map(
        expert_pass, (routed.reshape(stacked_shape), routed_cot.reshape(stacked_shape), w_gate, w_up, w_down))
    chosen = expert_output.reshape(buffer_rows, D)[target].astype(jnp.float32).reshape(TOKENS, TOPK, D)
    mixed = jnp.sum(route_weights[:, :, None] * chosen, axis=1).astype(jnp.bfloat16)
    grad_route = jnp.sum(cotangent.astype(jnp.float32)[:, None, :] * chosen, axis=2)
    chosen_grads = input_rows.reshape(buffer_rows, D)[target].astype(jnp.float32).reshape(TOKENS, TOPK, D)
    grad_tokens = jnp.sum(route_weights[:, :, None] * chosen_grads, axis=1).astype(jnp.bfloat16)
    return (mixed, grad_tokens, grad_route, grad_gate, grad_up, grad_down)
```

```python
import functools

import jax
import jax.numpy as jnp
from jax import lax
from jax.experimental import pallas as pl
from jax.experimental.pallas import tpu as pltpu
from jax.sharding import PartitionSpec as P

MESH = pl.DeviceIdType.MESH
F32 = jnp.float32
BF16 = jnp.bfloat16
NT_DIMS = (((1,), (1,)), ((), ()))
VMEM = pl.BlockSpec(memory_space=pltpu.VMEM)
ANY = pl.BlockSpec(memory_space=pl.ANY)


def remote(src, dst, send, recv, **where):
    return pltpu.make_async_remote_copy(
        src_ref=src, dst_ref=dst, send_sem=send, recv_sem=recv, device_id=where, device_id_type=MESH
    )


def wait_bytes(ref, sem):
    pltpu.make_async_copy(ref, ref, sem).wait()


def slot_rows(ids_col, ids_row, cap):
    n = ids_row.shape[1]
    earlier = lax.broadcasted_iota(jnp.int32, (n, n), 0) < lax.broadcasted_iota(jnp.int32, (n, n), 1)
    same_row = lax.broadcasted_iota(jnp.int32, (n, n), 0) == lax.broadcasted_iota(jnp.int32, (n, n), 1)
    targets = []
    for k in range(2):
        mine = ids_row[k : k + 1, :]
        count = jnp.zeros((1, n), F32)
        for other in range(2):
            before = earlier | same_row if other < k else earlier
            hit = (ids_col[:, other : other + 1] == mine) & before
            count = count + jnp.sum(jnp.where(hit, 1.0, 0.0), axis=0, keepdims=True)
        targets.append(mine.astype(F32) * cap + count)
    return targets


def slot_cols(ids_col, ids_row, cap):
    n = ids_row.shape[1]
    earlier = lax.broadcasted_iota(jnp.int32, (n, n), 1) < lax.broadcasted_iota(jnp.int32, (n, n), 0)
    same_row = lax.broadcasted_iota(jnp.int32, (n, n), 0) == lax.broadcasted_iota(jnp.int32, (n, n), 1)
    targets = []
    for k in range(2):
        mine = ids_col[:, k : k + 1]
        count = jnp.zeros((n, 1), F32)
        for other in range(2):
            before = earlier | same_row if other < k else earlier
            hit = (ids_row[other : other + 1, :] == mine) & before
            count = count + jnp.sum(jnp.where(hit, 1.0, 0.0), axis=1, keepdims=True)
        targets.append(mine.astype(F32) * cap + count)
    return targets


def greet(nx, nz, me, t):
    barrier = pltpu.get_barrier_semaphore()

    def hello(i, _):
        pl.semaphore_signal(
            barrier, inc=1, device_id={"expert": lax.rem(me + i, nx), "tensor": t}, device_id_type=MESH
        )
        return 0

    lax.fori_loop(1, nx, hello, 0)
    for step in (1, nz - 1):
        pl.semaphore_signal(
            barrier, inc=1, device_id={"expert": me, "tensor": lax.rem(t + step, nz)}, device_id_type=MESH
        )
    return barrier


PIECES = 2


def dispatch_kernel(
    nx, nz, cap,
    ids_col_ref, ids_row_ref, weight_ref, tok_ref, cot_ref,
    routed_ref, rcot_ref,
    sel_ref, tokbuf, tslots, cslots,
    ring_send, ring_recv, push_send, push_recv, self_sem, cpush_send, cpush_recv, cself_sem,
    cring_send, cring_recv,
):
    me, t = lax.axis_index("expert"), lax.axis_index("tensor")
    rows = nx * cap
    n_tok = tok_ref.shape[0]
    right, left = lax.rem(t + 1, nz), lax.rem(t + nz - 1, nz)
    barrier = greet(nx, nz, me, t)

    t0, t1 = slot_rows(ids_col_ref[...], ids_row_ref[...], cap)
    w0, w1 = weight_ref[0:1, :], weight_ref[1:2, :]
    tile = 128

    def select(i, _):
        r = pl.ds(pl.multiple_of(i * tile, tile), tile)
        at = (lax.broadcasted_iota(jnp.int32, (tile, n_tok), 0) + i * tile).astype(F32)
        hit0, hit1 = at == t0, at == t1
        sel = jnp.where(hit0 | hit1, 1.0, 0.0).astype(BF16)
        sel_ref[r, :] = sel
        w = jnp.sum(jnp.where(hit0, w0, 0.0) + jnp.where(hit1, w1, 0.0), axis=1, keepdims=True)
        cslots[r, :] = (w * jnp.dot(sel, cot_ref[...], preferred_element_type=F32)).astype(BF16)
        return 0

    lax.fori_loop(0, rows // tile, select, 0)

    def fill(o, block):
        def body(i, _):
            r = pl.ds(pl.multiple_of(i * tile, tile), tile)
            tslots[o, r, :] = jnp.dot(sel_ref[r, :], block[...], preferred_element_type=F32).astype(BF16)
            return 0

        lax.fori_loop(0, rows // tile, body, 0)

    fill(t, tok_ref)
    pl.semaphore_wait(barrier, nx + 1)

    def slab(e):
        return pl.ds(pl.multiple_of(e * cap, cap), cap)

    def ring_right(k):
        o = lax.rem(t + nz - k, nz)
        return remote(
            tok_ref if k == 0 else tokbuf.at[o], tokbuf.at[o], ring_send.at[0, k], ring_recv.at[0, k],
            expert=me, tensor=right,
        )

    def ring_left(k):
        o = lax.rem(t + k, nz)
        return remote(
            tok_ref if k == 0 else tokbuf.at[o], tokbuf.at[o], ring_send.at[1, k], ring_recv.at[1, k],
            expert=me, tensor=left,
        )

    hops_right, hops_left = nz // 2, nz - 1 - nz // 2
    started = [ring_right(0), ring_left(0)]
    for c in started:
        c.start()

    def push_cot(i, _):
        p = lax.rem(me + i, nx)
        remote(cslots.at[slab(p)], rcot_ref.at[t, slab(me)], cpush_send, cpush_recv, expert=p, tensor=t).start()
        return 0

    lax.fori_loop(1, nx, push_cot, 0)
    own_cot = pltpu.make_async_copy(cslots.at[slab(me)], rcot_ref.at[t, slab(me)], cself_sem)
    own_cot.start()

    def push_tok(o, k):
        def body(i, _):
            p = lax.rem(me + i, nx)
            remote(
                tslots.at[o, slab(p)], routed_ref.at[o, slab(me)], push_send.at[k], push_recv.at[k],
                expert=p, tensor=t,
            ).start()
            return 0

        lax.fori_loop(1, nx, body, 0)
        own = pltpu.make_async_copy(tslots.at[o, slab(me)], routed_ref.at[o, slab(me)], self_sem.at[k])
        own.start()
        return own

    def cot_right(k, p):
        o = lax.rem(t + nz - k, nz)
        size = rows // 2 // PIECES
        r = pl.ds(p * size, size)
        return remote(
            rcot_ref.at[o, r], rcot_ref.at[o, r], cring_send.at[0, k, p], cring_recv.at[0, k, p],
            expert=me, tensor=right,
        )

    def cot_left(k, p):
        o = lax.rem(t + k, nz)
        size = rows // 2 // PIECES
        r = pl.ds(rows // 2 + p * size, size)
        return remote(
            rcot_ref.at[o, r], rcot_ref.at[o, r], cring_send.at[1, k, p], cring_recv.at[1, k, p],
            expert=me, tensor=left,
        )

    owns = [push_tok(t, 0)]

    def token_step(k):
        got = [(ring_right, k, lax.rem(t + nz - k, nz), hops_right, k)]
        if k <= hops_left:
            got.append((ring_left, k, lax.rem(t + k, nz), hops_left, nz - k))
        for make, k, o, hops, index in got:
            make(k - 1).wait_recv()
            if k < hops:
                c = make(k)
                c.start()
                started.append(c)
        for make, k, o, hops, index in got:
            fill(o, tokbuf.at[o])
            owns.append(push_tok(o, index))

    def cot_step(k):
        for p in range(PIECES):
            for make in (cot_right, cot_left):
                if k > 0:
                    make(k - 1, p).wait_recv()
                if k < nz - 1:
                    c = make(k, p)
                    c.start()
                    started.append(c)

    token_step(1)
    wait_bytes(rcot_ref.at[0, pl.ds(0, rows - cap)], cpush_recv)
    own_cot.wait()
    cot_step(0)
    for k in range(2, hops_right + 1):
        token_step(k)
        cot_step(k - 1)
    for k in range(hops_right, nz):
        cot_step(k)

    for k in range(nz):
        owns[k].wait()
        wait_bytes(tslots.at[0, pl.ds(0, rows - cap)], push_send.at[k])
        wait_bytes(tslots.at[0, pl.ds(0, rows - cap)], push_recv.at[k])
    wait_bytes(cslots.at[pl.ds(0, rows - cap)], cpush_send)
    for c in started:
        c.wait_send()


def dispatch(nx, nz, cap, ids, ids_t, weights_t, tokens, cotangent):
    n_tok, width = tokens.shape
    rows = nx * cap
    dma = pltpu.SemaphoreType.DMA
    out = jax.ShapeDtypeStruct((nz, rows, width), BF16)
    return pl.pallas_call(
        functools.partial(dispatch_kernel, nx, nz, cap),
        out_shape=(out, out),
        in_specs=[VMEM] * 5,
        out_specs=(ANY, ANY),
        scratch_shapes=[
            pltpu.VMEM((rows, n_tok), BF16),
            pltpu.VMEM((nz, n_tok, width), BF16),
            pltpu.VMEM((nz, rows, width), BF16),
            pltpu.VMEM((rows, width), BF16),
            dma((2, nz // 2)), dma((2, nz // 2)), dma((nz,)), dma((nz,)), dma((nz,)), dma, dma, dma,
            dma((2, nz - 1, PIECES)), dma((2, nz - 1, PIECES)),
        ],
        compiler_params=pltpu.CompilerParams(
            collective_id=0, has_side_effects=True, vmem_limit_bytes=60 * 1024 * 1024
        ),
        name="dispatch",
    )(ids, ids_t, weights_t, tokens, cotangent)


def hidden_kernel(routed_ref, rcot_ref, wg_ref, wu_ref, wd_ref, hid_ref, dgu_ref, dot_ref, gu_acc, dh_acc):
    o = pl.program_id(0)
    w = jnp.concatenate([wg_ref[...], wu_ref[...]], axis=1)
    gu = jnp.dot(routed_ref[0], w, preferred_element_type=F32)
    dh = lax.dot_general(rcot_ref[0], wd_ref[...], NT_DIMS, preferred_element_type=F32)

    @pl.when(o == 0)
    def _():
        gu_acc[...] = gu
        dh_acc[...] = dh

    @pl.when(o > 0)
    def _():
        gu_acc[...] += gu
        dh_acc[...] += dh

    @pl.when(o == pl.num_programs(0) - 1)
    def _():
        h = dh_acc.shape[1]
        gate, up, d_hidden = gu_acc[:, :h], gu_acc[:, h:], dh_acc[...]
        sig = 1.0 / (1.0 + jnp.exp(-gate))
        silu = gate * sig
        hidden = (silu * up).astype(BF16)
        hid_ref[...] = hidden
        d_gate = d_hidden * up * sig * (1.0 + gate * (1.0 - sig))
        dgu_ref[...] = jnp.concatenate([d_gate.astype(BF16), (d_hidden * silu).astype(BF16)], axis=1)
        dot_ref[...] = jnp.sum(hidden.astype(F32) * d_hidden, axis=1, keepdims=True)


def hidden_stage(routed, rcot, wg, wu, wd):
    nz, rows, width = routed.shape
    h = wg.shape[1]
    block = pl.BlockSpec((1, rows, width), lambda o: (o, 0, 0))
    wspec = pl.BlockSpec((width, h), lambda o: (o, 0))
    return pl.pallas_call(
        hidden_kernel,
        grid=(nz,),
        out_shape=(
            jax.ShapeDtypeStruct((rows, h), BF16),
            jax.ShapeDtypeStruct((rows, 2 * h), BF16),
            jax.ShapeDtypeStruct((rows, 1), F32),
        ),
        in_specs=[block, block, wspec, wspec, pl.BlockSpec((h, width), lambda o: (0, o))],
        out_specs=[
            pl.BlockSpec((rows, h), lambda o: (0, 0)),
            pl.BlockSpec((rows, 2 * h), lambda o: (0, 0)),
            pl.BlockSpec((rows, 1), lambda o: (0, 0)),
        ],
        scratch_shapes=[pltpu.VMEM((rows, 2 * h), F32), pltpu.VMEM((rows, h), F32)],
        name="hidden",
    )(routed, rcot, wg, wu, wd)


def parts_kernel(hid_ref, dgu_ref, wg_ref, wu_ref, wd_ref, down_ref, back_ref):
    down_ref[0] = jnp.dot(hid_ref[...], wd_ref[...], preferred_element_type=F32).astype(BF16)
    w = jnp.concatenate([wg_ref[...], wu_ref[...]], axis=1)
    back_ref[0] = lax.dot_general(dgu_ref[...], w, NT_DIMS, preferred_element_type=F32).astype(BF16)


def parts_stage(nz, hid, dgu, wg, wu, wd):
    rows, h = hid.shape
    width = wg.shape[0] // nz
    out = jax.ShapeDtypeStruct((nz, rows, width), BF16)
    wspec = pl.BlockSpec((width, h), lambda o: (o, 0))
    block = pl.BlockSpec((1, rows, width), lambda o: (o, 0, 0))
    return pl.pallas_call(
        parts_kernel,
        grid=(nz,),
        out_shape=(out, out),
        in_specs=[
            pl.BlockSpec((rows, h), lambda o: (0, 0)),
            pl.BlockSpec((rows, 2 * h), lambda o: (0, 0)),
            wspec, wspec, pl.BlockSpec((h, width), lambda o: (0, o)),
        ],
        out_specs=(block, block),
        name="parts",
    )(hid, dgu, wg, wu, wd)


def grads_kernel(routed_ref, rcot_ref, hid_ref, dgu_ref, gg_ref, gu_ref, gd_ref, hid_t, dgu_t):
    @pl.when(pl.program_id(0) == 0)
    def _():
        hid_t[...] = hid_ref[...].astype(F32).T.astype(BF16)
        dgu_t[...] = dgu_ref[...].astype(F32).T.astype(BF16)

    h = hid_t.shape[0]
    gd_ref[...] = jnp.dot(hid_t[...], rcot_ref[0], preferred_element_type=F32).astype(BF16)
    both = jnp.dot(dgu_t[...], routed_ref[0], preferred_element_type=F32).T.astype(BF16)
    gg_ref[...] = both[:, :h]
    gu_ref[...] = both[:, h:]


def grads_stage(routed, rcot, hid, dgu):
    nz, rows, width = routed.shape
    h = hid.shape[1]
    block = pl.BlockSpec((1, rows, width), lambda o: (o, 0, 0))
    gspec = pl.BlockSpec((width, h), lambda o: (o, 0))
    return pl.pallas_call(
        grads_kernel,
        grid=(nz,),
        out_shape=(
            jax.ShapeDtypeStruct((nz * width, h), BF16),
            jax.ShapeDtypeStruct((nz * width, h), BF16),
            jax.ShapeDtypeStruct((h, nz * width), BF16),
        ),
        in_specs=[
            block, block,
            pl.BlockSpec((rows, h), lambda o: (0, 0)),
            pl.BlockSpec((rows, 2 * h), lambda o: (0, 0)),
        ],
        out_specs=(gspec, gspec, pl.BlockSpec((h, width), lambda o: (0, o))),
        scratch_shapes=[pltpu.VMEM((h, rows), BF16), pltpu.VMEM((2 * h, rows), BF16)],
        cost_estimate=pl.CostEstimate(
            flops=6 * nz * rows * width * h, bytes_accessed=4 * nz * rows * width + 6 * nz * width * h,
            transcendentals=0,
        ),
        name="grads",
    )(routed, rcot, hid, dgu)


def combine_kernel(cap, ids_col_ref, ids_row_ref, weight_ref, ret_ref, out_ref, pick):
    n = ids_col_ref.shape[0]
    rows = ret_ref.shape[1]

    @pl.when(pl.program_id(0) == 0)
    def _():
        at = lax.broadcasted_iota(jnp.int32, (n, rows), 1).astype(F32)
        for k, target in enumerate(slot_cols(ids_col_ref[...], ids_row_ref[...], cap)):
            pick[k * n : (k + 1) * n, :] = jnp.where(at == target, 1.0, 0.0).astype(BF16)

    chosen = jnp.dot(pick[...], ret_ref[0], preferred_element_type=F32)
    out_ref[0] = (weight_ref[:, 0:1] * chosen[:n] + weight_ref[:, 1:2] * chosen[n:]).astype(BF16)


def combine(cap, ids, ids_t, weights, ret):
    blocks, rows, width = ret.shape
    n = ids.shape[0]
    return pl.pallas_call(
        functools.partial(combine_kernel, cap),
        grid=(blocks,),
        out_shape=jax.ShapeDtypeStruct((blocks, n, width), BF16),
        in_specs=[
            pl.BlockSpec((n, 2), lambda o: (0, 0)),
            pl.BlockSpec((2, n), lambda o: (0, 0)),
            pl.BlockSpec((n, 2), lambda o: (0, 0)),
            pl.BlockSpec((1, rows, width), lambda o: (o, 0, 0)),
        ],
        out_specs=pl.BlockSpec((1, n, width), lambda o: (o, 0, 0)),
        scratch_shapes=[pltpu.VMEM((2 * n, rows), BF16)],
        name="combine",
    )(ids, ids_t, weights, ret)


def local(tokens, ids, weights, cotangent, w_gate, w_up, w_down):
    nx, nz = lax.axis_size("expert"), lax.axis_size("tensor")
    n_tok, width = tokens.shape
    cap = 4 * n_tok // nx
    ids_t, weights_t = ids.T, weights.T
    wg, wu, wd = w_gate[0], w_up[0], w_down[0]
    routed, rcot = dispatch(nx, nz, cap, ids, ids_t, weights_t, tokens, cotangent)
    hid, dgu, dots = hidden_stage(routed, rcot, wg, wu, wd)
    down, back = parts_stage(nz, hid, dgu, wg, wu, wd)

    returned = lax.all_to_all(
        down.reshape(nz, nx, cap, width), "expert", split_axis=1, concat_axis=1, tiled=True
    ).reshape(nz, nx * cap, width)
    input_rows = lax.psum_scatter(back, "tensor", scatter_dimension=0, tiled=True)
    dots_all = jnp.sum(lax.all_gather(dots[:, 0], "tensor", axis=0), axis=0)
    dots_back = lax.all_to_all(
        dots_all.reshape(nx, cap), "expert", split_axis=0, concat_axis=0, tiled=True
    ).reshape(nx * cap)
    ret_grads = lax.all_to_all(
        input_rows.reshape(nx, cap, width), "expert", split_axis=0, concat_axis=0, tiled=True
    ).reshape(1, nx * cap, width)
    grad_gate, grad_up, grad_down = grads_stage(routed, rcot, hid, dgu)
    mixed_parts = combine(cap, ids, ids_t, weights, returned)
    mixed = lax.psum_scatter(mixed_parts, "tensor", scatter_dimension=0, tiled=True)[0]
    grad_tokens = combine(cap, ids, ids_t, weights, ret_grads)[0]
    target = jnp.stack(slot_cols(ids, ids_t, cap), axis=1)[:, :, 0]
    at = jnp.arange(nx * cap, dtype=F32)
    grad_route = (
        jnp.sum(jnp.where(target[:, :, None] == at, dots_back, 0.0), axis=2) / weights
    )
    return (mixed, grad_tokens, grad_route, grad_gate[None], grad_up[None], grad_down[None])


def solution(mesh):
    placed = (
        P("expert", "tensor"),
        P("expert", None),
        P("expert", None),
        P("expert", "tensor"),
        P("expert", None, "tensor"),
        P("expert", None, "tensor"),
        P("expert", "tensor", None),
    )
    return jax.shard_map(
        local,
        mesh=mesh,
        in_specs=placed,
        out_specs=(
            P("expert", "tensor"),
            P("expert", "tensor"),
            P("expert", None),
            P("expert", None, "tensor"),
            P("expert", None, "tensor"),
            P("expert", "tensor", None),
        ),
        check_vma=False,
    )
```

```python
import functools

import jax
import jax.numpy as jnp
from jax import lax
from jax.experimental import pallas as pl
from jax.experimental.pallas import tpu as pltpu
from jax.sharding import PartitionSpec as P

MESH = pl.DeviceIdType.MESH
F32 = jnp.float32
BF16 = jnp.bfloat16
NT_DIMS = (((1,), (1,)), ((), ()))
VMEM = pl.BlockSpec(memory_space=pltpu.VMEM)
ANY = pl.BlockSpec(memory_space=pl.ANY)


def remote(src, dst, send, recv, **where):
    return pltpu.make_async_remote_copy(
        src_ref=src, dst_ref=dst, send_sem=send, recv_sem=recv, device_id=where, device_id_type=MESH
    )


def wait_bytes(ref, sem):
    pltpu.make_async_copy(ref, ref, sem).wait()


def columns_of(row):
    n = row.shape[1]
    return jnp.broadcast_to(row, (n, n)).T


def slot_targets(rows, cols, cap, axis):
    n = rows[0].shape[1]
    here = lax.broadcasted_iota(jnp.int32, (n, n), 1 - axis)
    there = lax.broadcasted_iota(jnp.int32, (n, n), axis)
    targets = []
    for k in range(2):
        mine, others = (rows, cols) if axis == 0 else (cols, rows)
        count = None
        for other in range(2):
            before = there <= here if other < k else there < here
            hit = (others[other] == mine[k]) & before
            seen = jnp.sum(jnp.where(hit, 1.0, 0.0), axis=axis, keepdims=True)
            count = seen if count is None else count + seen
        own = mine[k] if axis == 0 else mine[k][:, 0:1]
        targets.append(own * cap + count)
    return targets


PIECES = 2
RS_PIECES = 2


def layer_kernel(
    nx, nz, cap,
    ids_ref, w_row_ref, tok_ref, cot_ref, wg_hbm, wu_hbm, wd_hbm,
    routed_ref, rcot_ref, mixed_ref, gtok_ref, groute_ref, gg_ref, gu_ref, gd_ref,
    wg_ref, wu_ref, wd_ref, sel_ref, tokbuf, slots, cslots, gu_acc, dh_acc, hid_ref, dgu_ref, w_col_ref,
    pick, hid_t, dgu_t, ret, rs0, rs, bk, islots, gret, mixb, rs2_0, rs2, dsrc, dret, dpart, dsum,
    routed_v, rcot_v, ggu_v, gd_v,
    ring_send, ring_recv, tpush_send, tpush_recv, tself_sem, cpush_send, cpush_recv, cself_sem,
    cring_send, cring_recv, weight_sem,
    push_send, push_recv, self_sem, rs_send, rs_recv, g_send, g_recv, rs2_send, rs2_recv,
    d_send, d_recv, z_send, z_recv, load_sem, store_sem,
):
    me, t = lax.axis_index("expert"), lax.axis_index("tensor")
    n_tok, width = tok_ref.shape
    rows, h = hid_ref.shape
    half, thalf = rows // 2, n_tok // 2
    right, left = lax.rem(t + 1, nz), lax.rem(t + nz - 1, nz)
    tile = 128
    barrier = pltpu.get_barrier_semaphore()

    def hello(i, _):
        pl.semaphore_signal(
            barrier, inc=1, device_id={"expert": lax.rem(me + i, nx), "tensor": t}, device_id_type=MESH
        )
        return 0

    def hello_z(i, _):
        pl.semaphore_signal(
            barrier, inc=1, device_id={"expert": me, "tensor": lax.rem(t + i, nz)}, device_id_type=MESH
        )
        return 0

    lax.fori_loop(1, nx, hello, 0)
    lax.fori_loop(1, nz, hello_z, 0)
    weight_loads = [
        pltpu.make_async_copy(src, dst, weight_sem.at[i])
        for i, (src, dst) in enumerate(((wg_hbm, wg_ref), (wu_hbm, wu_ref), (wd_hbm, wd_ref)))
    ]
    for c in weight_loads:
        c.start()

    def slab(e):
        return pl.ds(pl.multiple_of(e * cap, cap), cap)

    def at(step):
        return lax.rem(t + 2 * nz + step, nz)

    order = [-1, 1]
    for j in range(2, nz // 2):
        order += [-j, j]
    order += [nz // 2, 0]
    started = []

    def go(c):
        c.start()
        started.append(c)

    id_rows = [ids_ref[k : k + 1, :].astype(F32) for k in range(2)]
    id_cols = [columns_of(r) for r in id_rows]
    row_targets = slot_targets(id_rows, id_cols, cap, 0)
    w0, w1 = w_row_ref[0:1, :], w_row_ref[1:2, :]
    for k in range(2):
        w_col_ref[:, k : k + 1] = columns_of(w_row_ref[k : k + 1, :])[:, 0:1]

    def select(i, _):
        r = pl.ds(pl.multiple_of(i * tile, tile), tile)
        j = (lax.broadcasted_iota(jnp.int32, (tile, n_tok), 0) + i * tile).astype(F32)
        hit0, hit1 = j == row_targets[0], j == row_targets[1]
        sel = jnp.where(hit0 | hit1, 1.0, 0.0).astype(BF16)
        sel_ref[r, :] = sel
        w = jnp.sum(jnp.where(hit0, w0, 0.0) + jnp.where(hit1, w1, 0.0), axis=1, keepdims=True)
        cslots[r, :] = (w * jnp.dot(sel, cot_ref[...], preferred_element_type=F32)).astype(BF16)
        return 0

    lax.fori_loop(0, rows // tile, select, 0)

    def fill(o, block):
        def body(i, _):
            r = pl.ds(pl.multiple_of(i * tile, tile), tile)
            slots[o, r, :] = jnp.dot(sel_ref[r, :], block[...], preferred_element_type=F32).astype(BF16)
            return 0

        lax.fori_loop(0, rows // tile, body, 0)

    pl.semaphore_wait(barrier, nx + nz - 2)

    def ring(d, k):
        o = at((-k, k)[d])
        return remote(
            tok_ref if k == 0 else tokbuf.at[o], tokbuf.at[o], ring_send.at[d, k], ring_recv.at[d, k],
            expert=me, tensor=(right, left)[d],
        )

    ring_hops = (nz // 2, nz - 1 - nz // 2)
    go(ring(0, 0))
    go(ring(1, 0))

    def push_cot(i, _):
        q = lax.rem(me + i, nx)
        remote(cslots.at[slab(q)], rcot_ref.at[t, slab(me)], cpush_send, cpush_recv, expert=q, tensor=t).start()
        return 0

    lax.fori_loop(1, nx, push_cot, 0)
    own_cot = pltpu.make_async_copy(cslots.at[slab(me)], rcot_ref.at[t, slab(me)], cself_sem)
    own_cot.start()
    token_order, token_owns = [], []

    def push_tok(step):
        i, o = len(token_order), at(step)

        def body(j, _):
            q = lax.rem(me + j, nx)
            remote(
                slots.at[o, slab(q)], routed_ref.at[o, slab(me)], tpush_send.at[i], tpush_recv.at[i],
                expert=q, tensor=t,
            ).start()
            return 0

        lax.fori_loop(1, nx, body, 0)
        own = pltpu.make_async_copy(slots.at[o, slab(me)], routed_ref.at[o, slab(me)], tself_sem.at[i])
        own.start()
        token_owns.append(own)
        token_order.append(step)

    def cot_ring(d, k, p):
        o, size = at((-k, k)[d]), half // PIECES
        r = pl.ds(d * half + p * size, size)
        return remote(
            rcot_ref.at[o, r], rcot_ref.at[o, r], cring_send.at[d, k, p], cring_recv.at[d, k, p],
            expert=me, tensor=(right, left)[d],
        )

    def token_step(k):
        came = [d for d in range(2) if k <= ring_hops[d]]
        for d in came:
            ring(d, k - 1).wait_recv()
            if k < ring_hops[d]:
                go(ring(d, k))
        for d in came:
            step = (-k, k)[d]
            fill(at(step), tokbuf.at[at(step)])
            push_tok(step)

    def cot_step(k):
        for p in range(PIECES):
            for d in range(2):
                if k > 0:
                    cot_ring(d, k - 1, p).wait_recv()
                if k < nz - 1:
                    go(cot_ring(d, k, p))

    def half_load(d, k):
        r = pl.ds(d * half, half)
        return pltpu.make_async_copy(
            rcot_ref.at[at((-k, k)[d]), r], rcot_v.at[k % 2, r], load_sem.at[d, k % 2]
        )

    def start_cot(k):
        for d in range(2):
            half_load(d, k).start()

    def add_cot(k):
        for d in range(2):
            r = pl.ds(d * half, half)
            half_load(d, k).wait()
            cols = pl.ds(pl.multiple_of(at((-k, k)[d]) * width, 128), width)
            dh = lax.dot_general(rcot_v[k % 2, r, :], wd_ref[:, cols], NT_DIMS, preferred_element_type=F32)
            dh_acc[r, :] = dh if k == 0 else dh_acc[r, :] + dh

    def tok_load(i):
        return pltpu.make_async_copy(routed_ref.at[at(token_order[i])], routed_v.at[i % 2], tself_sem.at[i])

    def start_tok(i):
        token_owns[i].wait()
        wait_bytes(slots.at[0, pl.ds(0, rows - cap)], tpush_recv.at[i])
        tok_load(i).start()

    def add_tok(i):
        tok_load(i).wait()
        w = weight_block(at(token_order[i]))
        for j in range(rows // tile):
            r = pl.ds(j * tile, tile)
            gu = jnp.dot(routed_v[i % 2, r, :], w, preferred_element_type=F32)
            gu_acc[r, :] = gu if i == 0 else gu_acc[r, :] + gu

    def weight_block(o):
        r = pl.ds(pl.multiple_of(o * width, 128), width)
        return jnp.concatenate([wg_ref[r, :], wu_ref[r, :]], axis=1)

    def fill_bk(d, o, into):
        w = weight_block(o)
        for i in range(half // tile):
            lhs = dgu_ref[pl.ds(d * half + i * tile, tile), :]
            into[d, pl.ds(i * tile, tile), :] = lax.dot_general(
                lhs, w, NT_DIMS, preferred_element_type=F32
            ).astype(into.dtype)

    def rs_copy(k, d, p):
        size = half // RS_PIECES
        r = pl.ds(p * size, size)
        return remote(
            rs0.at[d, r] if k == 0 else rs.at[d, k - 1, r], rs.at[d, k, r],
            rs_send.at[d, k, p], rs_recv.at[d, k, p], expert=me, tensor=(right, left)[d],
        )

    fill(t, tok_ref)
    push_tok(0)
    token_step(1)
    wait_bytes(cslots.at[pl.ds(0, rows - cap)], cpush_recv)
    own_cot.wait()
    cot_step(0)
    start_cot(0)
    token_step(2)
    cot_step(1)
    for c in weight_loads:
        c.wait()
    add_cot(0)
    start_cot(1)
    token_step(3)
    cot_step(2)
    add_cot(1)
    start_cot(2)
    token_step(4)
    cot_step(3)
    start_tok(0)
    add_cot(2)
    start_cot(3)
    add_tok(0)
    cot_step(4)
    start_tok(1)
    add_cot(3)
    start_cot(4)
    add_tok(1)
    cot_step(5)
    start_tok(2)
    add_cot(4)
    start_cot(5)
    add_tok(2)
    cot_step(6)
    start_tok(3)
    add_cot(5)
    start_cot(6)
    add_tok(3)
    start_tok(4)
    add_cot(6)
    cot_step(7)
    start_cot(7)
    add_tok(4)
    start_tok(5)
    add_cot(7)
    add_tok(5)
    start_tok(6)
    add_tok(6)
    lanes = lax.broadcasted_iota(jnp.int32, (n_tok, rows), 1).astype(F32)
    for k, target in enumerate(slot_targets(id_rows, id_cols, cap, 1)):
        pick[pl.ds(k * n_tok, n_tok), :] = jnp.where(lanes == target, 1.0, 0.0).astype(BF16)
    start_tok(7)
    add_tok(7)
    for i in range(nz):
        wait_bytes(slots.at[0, pl.ds(0, rows - cap)], tpush_send.at[i])

    for j in range(rows // tile):
        r = pl.ds(j * tile, tile)
        gate, up, d_hidden = gu_acc[r, :h], gu_acc[r, h:], dh_acc[r, :]
        sig = 1.0 / (1.0 + jnp.exp(-gate))
        silu = gate * sig
        hidden = (silu * up).astype(BF16)
        hid_ref[r, :] = hidden
        dgu_ref[r, :h] = (d_hidden * up * sig * (1.0 + gate * (1.0 - sig))).astype(BF16)
        dgu_ref[r, h:] = (d_hidden * silu).astype(BF16)
        dots = jnp.sum(hidden.astype(F32) * d_hidden, axis=1, keepdims=True)
        dsrc[r, :] = jnp.broadcast_to(dots, (tile, dsrc.shape[1]))


    def push_dots(i, _):
        q = lax.rem(me + i, nx)
        remote(dsrc.at[slab(q)], dret.at[slab(me)], d_send, d_recv, expert=q, tensor=t).start()
        return 0

    owns = []

    def down(i):
        o = at(order[i])
        cols = pl.ds(pl.multiple_of(o * width, 128), width)

        def body(j, _):
            r = pl.ds(pl.multiple_of(j * tile, tile), tile)
            slots[o, r, :] = jnp.dot(hid_ref[r, :], wd_ref[:, cols], preferred_element_type=F32).astype(BF16)
            return 0

        lax.fori_loop(0, rows // tile, body, 0)

        def push(j, _):
            q = lax.rem(me + j, nx)
            remote(
                slots.at[o, slab(q)], ret.at[o, slab(me)], push_send.at[i], push_recv.at[i], expert=q, tensor=t
            ).start()
            return 0

        lax.fori_loop(1, nx, push, 0)
        own = pltpu.make_async_copy(slots.at[o, slab(me)], ret.at[o, slab(me)], self_sem.at[i])
        own.start()
        owns.append(own)

    down(0)
    fill_bk(0, at(-1), rs0)
    fill_bk(1, at(1), rs0)
    for p in range(RS_PIECES):
        for d in range(2):
            go(rs_copy(0, d, p))
    lax.fori_loop(1, nx, push_dots, 0)
    dret[slab(me), :] = dsrc[slab(me), :]
    down(1)

    hid_t[...] = hid_ref[...].astype(F32).T.astype(BF16)
    dgu_t[...] = dgu_ref[...].astype(F32).T.astype(BF16)

    def load(o):
        return (
            pltpu.make_async_copy(routed_ref.at[o], routed_v.at[o % 2], load_sem.at[0, o % 2]),
            pltpu.make_async_copy(rcot_ref.at[o], rcot_v.at[o % 2], load_sem.at[1, o % 2]),
        )

    def store(o):
        r = pl.ds(o * width, width)
        return (
            pltpu.make_async_copy(ggu_v.at[o % 2, 0], gg_ref.at[r], store_sem.at[0, o % 2]),
            pltpu.make_async_copy(ggu_v.at[o % 2, 1], gu_ref.at[r], store_sem.at[1, o % 2]),
            pltpu.make_async_copy(gd_v.at[o % 2], gd_ref.at[:, r], store_sem.at[2, o % 2]),
        )

    for c in load(0):
        c.start()

    def grads(o):
        for c in load(o):
            c.wait()
        if o + 1 < nz:
            for c in load(o + 1):
                c.start()
        if o >= 2:
            for c in store(o - 2):
                c.wait()
        s = o % 2
        gd_v[s] = jnp.dot(hid_t[...], rcot_v[s], preferred_element_type=F32).astype(BF16)
        both = jnp.dot(dgu_t[...], routed_v[s], preferred_element_type=F32).T.astype(BF16)
        ggu_v[s, 0] = both[:, :h]
        ggu_v[s, 1] = both[:, h:]
        for c in store(o):
            c.start()

    def mix(i):
        o = at(order[i])
        owns[i].wait()
        wait_bytes(ret.at[0, pl.ds(0, rows - cap)], push_recv.at[i])
        chosen = jnp.dot(pick[...], ret[o], preferred_element_type=F32)
        mixb[o] = w_col_ref[:, 0:1] * chosen[:n_tok] + w_col_ref[:, 1:2] * chosen[n_tok:]

    def rs2_copy(k, d):
        return remote(
            rs2_0.at[d] if k == 0 else rs2.at[d, k - 1], rs2.at[d, k],
            rs2_send.at[d, k], rs2_recv.at[d, k], expert=me, tensor=(right, left)[d],
        )

    def rs2_step(k):
        for d in range(2):
            o = at((-1 - k, 1 + k)[d])
            part = mixb[o, pl.ds(d * thalf, thalf), :]
            if k == 0:
                rs2_0[d] = part.astype(BF16)
            else:
                rs2_copy(k - 1, d).wait_recv()
                part = rs2[d, k - 1].astype(F32) + part
                if k < nz - 1:
                    rs2[d, k - 1] = part.astype(BF16)
                else:
                    mixed_ref[pl.ds(d * thalf, thalf), :] = part.astype(BF16)
            if k < nz - 1:
                go(rs2_copy(k, d))

    def route_part():
        wait_bytes(dret.at[pl.ds(0, rows - cap)], d_recv)
        j = lax.broadcasted_iota(jnp.int32, (rows, n_tok), 0).astype(F32)
        dpart[...] = jnp.zeros_like(dpart)
        for k, target in enumerate(row_targets):
            dpart[k : k + 1, :] = jnp.sum(jnp.where(j == target, dret[...], 0.0), axis=0, keepdims=True)

        def share(i, _):
            remote(dpart, dsum.at[t], z_send, z_recv, expert=me, tensor=lax.rem(t + i, nz)).start()
            return 0

        lax.fori_loop(1, nz, share, 0)
        dsum[t] = dpart[...]

    size = half // RS_PIECES
    for k in range(1, nz):
        for d in range(2):
            fill_bk(d, at((-1 - k, 1 + k)[d]), bk)
        if k + 1 < nz:
            down(k + 1)
        for p in range(RS_PIECES):
            r = pl.ds(p * size, size)
            for d in range(2):
                rs_copy(k - 1, d, p).wait_recv()
                total = (rs[d, k - 1, r, :].astype(F32) + bk[d, r, :]).astype(BF16)
                if k < nz - 1:
                    rs[d, k - 1, r, :] = total
                    go(rs_copy(k, d, p))
                    continue
                islots[pl.ds(d * half + p * size, size), :] = total
                first, count = (d * half + p * size) // cap, size // cap

                def push_grad(i, _):
                    q = first + lax.rem(me + i, count)

                    @pl.when(q != me)
                    def _():
                        remote(islots.at[slab(q)], gret.at[slab(me)], g_send, g_recv, expert=q, tensor=t).start()

                    return 0

                lax.fori_loop(0, count, push_grad, 0)
        grads(k - 1)
        if k >= 2:
            mix(k - 2)
        if k == 2:
            route_part()
        if k in (3, 5, 7):
            rs2_step((k - 3) // 2)
    gret[slab(me), :] = islots[slab(me), :]
    grads(nz - 1)
    mix(nz - 2)
    for k in range(3, nz - 1):
        rs2_step(k)
    mix(nz - 1)
    wait_bytes(gret.at[pl.ds(0, rows - cap)], g_recv)
    chosen = jnp.dot(pick[...], gret[...], preferred_element_type=F32)
    gtok_ref[...] = (w_col_ref[:, 0:1] * chosen[:n_tok] + w_col_ref[:, 1:2] * chosen[n_tok:]).astype(BF16)
    rs2_step(nz - 1)

    wait_bytes(dsum.at[pl.ds(0, nz - 1)], z_recv)
    total = dsum[0]
    for z in range(1, nz):
        total = total + dsum[z]
    groute_ref[...] = total[0:2, :] / w_row_ref[...]

    for o in (nz - 2, nz - 1):
        for c in store(o):
            c.wait()
    for c in started:
        c.wait_send()
    for i in range(nz):
        wait_bytes(slots.at[0, pl.ds(0, rows - cap)], push_send.at[i])
    wait_bytes(islots.at[pl.ds(0, rows - cap)], g_send)
    wait_bytes(dsrc.at[pl.ds(0, rows - cap)], d_send)
    wait_bytes(dsum.at[pl.ds(0, nz - 1)], z_send)
    wait_bytes(cslots.at[pl.ds(0, rows - cap)], cpush_send)


def layer(nx, nz, cap, ids_t, weights_t, tokens, cotangent, wg, wu, wd):
    n_tok, width = tokens.shape
    h = wg.shape[1]
    rows = nx * cap
    dma = pltpu.SemaphoreType.DMA
    small = jax.ShapeDtypeStruct((n_tok, width), BF16)
    tall = jax.ShapeDtypeStruct((nz * width, h), BF16)
    buffer = jax.ShapeDtypeStruct((nz, rows, width), BF16)
    return pl.pallas_call(
        functools.partial(layer_kernel, nx, nz, cap),
        out_shape=(
            buffer, buffer, small, small, jax.ShapeDtypeStruct((2, n_tok), F32), tall, tall,
            jax.ShapeDtypeStruct((h, nz * width), BF16),
        ),
        in_specs=[VMEM] * 4 + [ANY] * 3,
        out_specs=(ANY, ANY, VMEM, VMEM, VMEM, ANY, ANY, ANY),
        scratch_shapes=[
            pltpu.VMEM((nz * width, h), BF16),
            pltpu.VMEM((nz * width, h), BF16),
            pltpu.VMEM((h, nz * width), BF16),
            pltpu.VMEM((rows, n_tok), BF16),
            pltpu.VMEM((nz, n_tok, width), BF16),
            pltpu.VMEM((nz, rows, width), BF16),
            pltpu.VMEM((rows, width), BF16),
            pltpu.VMEM((rows, 2 * h), F32),
            pltpu.VMEM((rows, h), F32),
            pltpu.VMEM((rows, h), BF16),
            pltpu.VMEM((rows, 2 * h), BF16),
            pltpu.VMEM((n_tok, 2), F32),
            pltpu.VMEM((2 * n_tok, rows), BF16),
            pltpu.VMEM((h, rows), BF16),
            pltpu.VMEM((2 * h, rows), BF16),
            pltpu.VMEM((nz, rows, width), BF16),
            pltpu.VMEM((2, rows // 2, width), BF16),
            pltpu.VMEM((2, nz - 1, rows // 2, width), BF16),
            pltpu.VMEM((2, rows // 2, width), F32),
            pltpu.VMEM((rows, width), BF16),
            pltpu.VMEM((rows, width), BF16),
            pltpu.VMEM((nz, n_tok, width), F32),
            pltpu.VMEM((2, n_tok // 2, width), BF16),
            pltpu.VMEM((2, nz - 1, n_tok // 2, width), BF16),
            pltpu.VMEM((rows, 128), F32),
            pltpu.VMEM((rows, 128), F32),
            pltpu.VMEM((8, n_tok), F32),
            pltpu.VMEM((nz, 8, n_tok), F32),
            pltpu.VMEM((2, rows, width), BF16),
            pltpu.VMEM((2, rows, width), BF16),
            pltpu.VMEM((2, 2, width, h), BF16),
            pltpu.VMEM((2, h, width), BF16),
            dma((2, nz // 2)), dma((2, nz // 2)), dma((nz,)), dma((nz,)), dma((nz,)), dma, dma, dma,
            dma((2, nz - 1, PIECES)), dma((2, nz - 1, PIECES)), dma((3,)),
            dma((nz,)), dma((nz,)), dma((nz,)),
            dma((2, nz - 1, RS_PIECES)), dma((2, nz - 1, RS_PIECES)),
            dma, dma, dma((2, nz - 1)), dma((2, nz - 1)),
            dma, dma, dma, dma, dma((2, 2)), dma((3, 2)),
        ],
        compiler_params=pltpu.CompilerParams(
            collective_id=0, has_side_effects=True, vmem_limit_bytes=62 * 1024 * 1024
        ),
        name="layer",
    )(ids_t, weights_t, tokens, cotangent, wg, wu, wd)


def local(tokens, ids, weights, cotangent, w_gate, w_up, w_down):
    nx, nz = lax.axis_size("expert"), lax.axis_size("tensor")
    cap = 4 * tokens.shape[0] // nx
    _, _, mixed, grad_tokens, grad_route, grad_gate, grad_up, grad_down = layer(
        nx, nz, cap, ids.T, weights.T, tokens, cotangent, w_gate[0], w_up[0], w_down[0]
    )
    return (mixed, grad_tokens, grad_route.T, grad_gate[None], grad_up[None], grad_down[None])


def solution(mesh):
    placed = (
        P("expert", "tensor"),
        P("expert", None),
        P("expert", None),
        P("expert", "tensor"),
        P("expert", None, "tensor"),
        P("expert", None, "tensor"),
        P("expert", "tensor", None),
    )
    return jax.shard_map(
        local,
        mesh=mesh,
        in_specs=placed,
        out_specs=(
            P("expert", "tensor"),
            P("expert", "tensor"),
            P("expert", None),
            P("expert", None, "tensor"),
            P("expert", None, "tensor"),
            P("expert", "tensor", None),
        ),
        check_vma=False,
    )
```

```python
import functools

import jax
import jax.numpy as jnp
from jax import lax
from jax.experimental import pallas as pl
from jax.experimental.pallas import tpu as pltpu
from jax.sharding import PartitionSpec as P

MESH = pl.DeviceIdType.MESH
F32 = jnp.float32
BF16 = jnp.bfloat16
NT_DIMS = (((1,), (1,)), ((), ()))
VMEM = pl.BlockSpec(memory_space=pltpu.VMEM)
ANY = pl.BlockSpec(memory_space=pl.ANY)


def remote(src, dst, send, recv, **where):
    return pltpu.make_async_remote_copy(
        src_ref=src, dst_ref=dst, send_sem=send, recv_sem=recv, device_id=where, device_id_type=MESH
    )


def wait_bytes(ref, sem):
    pltpu.make_async_copy(ref, ref, sem).wait()


def columns_of(row):
    n = row.shape[1]
    return jnp.broadcast_to(row, (n, n)).T


def slot_targets(rows, cols, cap, axis):
    n = rows[0].shape[1]
    here = lax.broadcasted_iota(jnp.int32, (n, n), 1 - axis)
    there = lax.broadcasted_iota(jnp.int32, (n, n), axis)
    targets = []
    for k in range(2):
        mine, others = (rows, cols) if axis == 0 else (cols, rows)
        count = None
        for other in range(2):
            before = there <= here if other < k else there < here
            hit = (others[other] == mine[k]) & before
            seen = jnp.sum(jnp.where(hit, 1.0, 0.0), axis=axis, keepdims=True)
            count = seen if count is None else count + seen
        own = mine[k] if axis == 0 else mine[k][:, 0:1]
        targets.append(own * cap + count)
    return targets


PIECES = 2
RS_PIECES = 2
RS2_LAG = 4


def layer_kernel(
    nx, nz, cap,
    ids_ref, w_row_ref, tok_ref, cot_ref, wg_hbm, wu_hbm, wd_hbm,
    routed_ref, rcot_ref, mixed_ref, gtok_ref, groute_ref, gg_ref, gu_ref, gd_ref,
    wg_ref, wu_ref, wd_ref, sel_ref, tokbuf, slots, cslots, gu_acc, dh_acc, hid_ref, dgu_ref, w_col_ref,
    pick, hid_t, dgu_t, ret, rs0, rs, bk, islots, gret, mix_v, rs2_0, rs2, dsrc, dret, dpart, dsum,
    routed_v, rcot_v, ggu_v, gd_v,
    ring_send, ring_recv, tpush_send, tpush_recv, tself_sem, cpush_send, cpush_recv, cself_sem,
    cring_send, cring_recv, cload_sem, weight_sem,
    push_send, push_recv, self_sem, rs_send, rs_recv, g_send, g_recv, rs2_send, rs2_recv,
    d_send, d_recv, z_send, z_recv, load_sem, store_sem,
):
    me, t = lax.axis_index("expert"), lax.axis_index("tensor")
    n_tok, width = tok_ref.shape
    rows, h = hid_ref.shape
    half, thalf = rows // 2, n_tok // 2
    right, left = lax.rem(t + 1, nz), lax.rem(t + nz - 1, nz)
    tile = 128
    barrier = pltpu.get_barrier_semaphore()

    def hello(i, _):
        pl.semaphore_signal(
            barrier, inc=1, device_id={"expert": lax.rem(me + i, nx), "tensor": t}, device_id_type=MESH
        )
        return 0

    def hello_z(i, _):
        pl.semaphore_signal(
            barrier, inc=1, device_id={"expert": me, "tensor": lax.rem(t + i, nz)}, device_id_type=MESH
        )
        return 0

    lax.fori_loop(1, nx, hello, 0)
    lax.fori_loop(1, nz, hello_z, 0)
    weight_loads = [
        pltpu.make_async_copy(src, dst, weight_sem.at[i])
        for i, (src, dst) in enumerate(((wg_hbm, wg_ref), (wu_hbm, wu_ref), (wd_hbm, wd_ref)))
    ]
    for c in weight_loads:
        c.start()

    def slab(e):
        return pl.ds(pl.multiple_of(e * cap, cap), cap)

    def at(step):
        return lax.rem(t + 2 * nz + step, nz)

    started = []

    def go(c):
        c.start()
        started.append(c)

    id_rows = [ids_ref[k : k + 1, :].astype(F32) for k in range(2)]
    id_cols = [columns_of(r) for r in id_rows]
    row_targets = slot_targets(id_rows, id_cols, cap, 0)
    w0, w1 = w_row_ref[0:1, :], w_row_ref[1:2, :]
    for k in range(2):
        w_col_ref[:, k : k + 1] = columns_of(w_row_ref[k : k + 1, :])[:, 0:1]

    def select(i, _):
        r = pl.ds(pl.multiple_of(i * tile, tile), tile)
        j = (lax.broadcasted_iota(jnp.int32, (tile, n_tok), 0) + i * tile).astype(F32)
        hit0, hit1 = j == row_targets[0], j == row_targets[1]
        sel = jnp.where(hit0 | hit1, 1.0, 0.0).astype(BF16)
        sel_ref[r, :] = sel
        w = jnp.sum(jnp.where(hit0, w0, 0.0) + jnp.where(hit1, w1, 0.0), axis=1, keepdims=True)
        cslots[r, :] = (w * jnp.dot(sel, cot_ref[...], preferred_element_type=F32)).astype(BF16)
        return 0

    lax.fori_loop(0, rows // tile, select, 0)

    def fill(o, block):
        def body(i, _):
            r = pl.ds(pl.multiple_of(i * tile, tile), tile)
            slots[o, r, :] = jnp.dot(sel_ref[r, :], block[...], preferred_element_type=F32).astype(BF16)
            return 0

        lax.fori_loop(0, rows // tile, body, 0)

    fill(t, tok_ref)
    pl.semaphore_wait(barrier, nx + nz - 2)

    def ring(d, k, p):
        o, size = at((-k, k)[d]), n_tok // PIECES
        r = pl.ds(p * size, size)
        return remote(
            tok_ref.at[r] if k == 0 else tokbuf.at[o, r], tokbuf.at[o, r],
            ring_send.at[d, k, p], ring_recv.at[d, k, p], expert=me, tensor=(right, left)[d],
        )

    ring_hops = (nz // 2, nz - 1 - nz // 2)
    for p in range(PIECES):
        for d in range(2):
            go(ring(d, 0, p))

    def push_cot(i, _):
        q = lax.rem(me + i, nx)
        remote(cslots.at[slab(q)], rcot_ref.at[t, slab(me)], cpush_send, cpush_recv, expert=q, tensor=t).start()
        return 0

    lax.fori_loop(1, nx, push_cot, 0)
    own_cot = pltpu.make_async_copy(cslots.at[slab(me)], rcot_ref.at[t, slab(me)], cself_sem)
    own_cot.start()
    token_order, token_owns = [], []

    def push_tok(step):
        i, o = len(token_order), at(step)

        def body(j, _):
            q = lax.rem(me + j, nx)
            remote(
                slots.at[o, slab(q)], routed_ref.at[o, slab(me)], tpush_send.at[i], tpush_recv.at[i],
                expert=q, tensor=t,
            ).start()
            return 0

        lax.fori_loop(1, nx, body, 0)
        own = pltpu.make_async_copy(slots.at[o, slab(me)], routed_ref.at[o, slab(me)], tself_sem.at[i])
        own.start()
        token_owns.append(own)
        token_order.append(step)

    def cot_ring(d, k, p):
        o, size = at((-k, k)[d]), half // PIECES
        r = pl.ds(d * half + p * size, size)
        return remote(
            rcot_ref.at[o, r], rcot_ref.at[o, r], cring_send.at[d, k, p], cring_recv.at[d, k, p],
            expert=me, tensor=(right, left)[d],
        )

    def token_step(k):
        came = [d for d in range(2) if k <= ring_hops[d]]
        for p in range(PIECES):
            for d in came:
                ring(d, k - 1, p).wait_recv()
                if k < ring_hops[d]:
                    go(ring(d, k, p))
        for d in came:
            step = (-k, k)[d]
            fill(at(step), tokbuf.at[at(step)])
            push_tok(step)

    def cot_load(d, k, p):
        size = half // PIECES
        r = pl.ds(d * half + p * size, size)
        return pltpu.make_async_copy(
            rcot_ref.at[at((-k, k)[d]), r], rcot_v.at[k % 2, r], cload_sem.at[d, k % 2, p]
        )

    def cot_step(k):
        for p in range(PIECES):
            for d in range(2):
                if k > 0:
                    cot_ring(d, k - 1, p).wait_recv()
                if k < nz - 1:
                    go(cot_ring(d, k, p))
                cot_load(d, k, p).start()

    def add_cot(k):
        for d in range(2):
            r = pl.ds(d * half, half)
            for p in range(PIECES):
                cot_load(d, k, p).wait()
            cols = pl.ds(pl.multiple_of(at((-k, k)[d]) * width, 128), width)
            dh = lax.dot_general(rcot_v[k % 2, r, :], wd_ref[:, cols], NT_DIMS, preferred_element_type=F32)
            dh_acc[r, :] = dh if k == 0 else dh_acc[r, :] + dh

    def tok_load(i):
        return pltpu.make_async_copy(routed_ref.at[at(token_order[i])], routed_v.at[i % 2], tself_sem.at[i])

    def start_tok(i):
        token_owns[i].wait()
        wait_bytes(slots.at[0, pl.ds(0, rows - cap)], tpush_recv.at[i])
        tok_load(i).start()

    def add_tok(i):
        tok_load(i).wait()
        w = weight_block(at(token_order[i]))
        for j in range(rows // tile):
            r = pl.ds(j * tile, tile)
            gu = jnp.dot(routed_v[i % 2, r, :], w, preferred_element_type=F32)
            gu_acc[r, :] = gu if i == 0 else gu_acc[r, :] + gu

    def weight_block(o):
        r = pl.ds(pl.multiple_of(o * width, 128), width)
        return jnp.concatenate([wg_ref[r, :], wu_ref[r, :]], axis=1)

    def fill_bk(d, o, into):
        w = weight_block(o)
        for i in range(half // tile):
            lhs = dgu_ref[pl.ds(d * half + i * tile, tile), :]
            into[d, pl.ds(i * tile, tile), :] = lax.dot_general(
                lhs, w, NT_DIMS, preferred_element_type=F32
            ).astype(into.dtype)

    def rs_copy(k, d, p):
        size = half // RS_PIECES
        r = pl.ds(p * size, size)
        return remote(
            rs0.at[d, r] if k == 0 else rs.at[d, k - 1, r], rs.at[d, k, r],
            rs_send.at[d, k, p], rs_recv.at[d, k, p], expert=me, tensor=(right, left)[d],
        )

    push_tok(0)
    token_step(1)
    wait_bytes(cslots.at[pl.ds(0, rows - cap)], cpush_recv)
    own_cot.wait()
    cot_step(0)
    token_step(2)
    cot_step(1)
    for c in weight_loads:
        c.wait()
    add_cot(0)
    token_step(3)
    cot_step(2)
    add_cot(1)
    token_step(4)
    cot_step(3)
    start_tok(0)
    add_cot(2)
    start_tok(1)
    add_tok(0)
    cot_step(4)
    start_tok(2)
    add_cot(3)
    add_tok(1)
    start_tok(3)
    add_tok(2)
    cot_step(5)
    start_tok(4)
    add_cot(4)
    add_tok(3)
    start_tok(5)
    add_tok(4)
    cot_step(6)
    start_tok(6)
    add_cot(5)
    add_tok(5)
    add_tok(6)
    add_cot(6)
    lanes = lax.broadcasted_iota(jnp.int32, (n_tok, rows), 1).astype(F32)
    for k, target in enumerate(slot_targets(id_rows, id_cols, cap, 1)):
        pick[pl.ds(k * n_tok, n_tok), :] = jnp.where(lanes == target, 1.0, 0.0).astype(BF16)
    start_tok(7)
    add_tok(7)

    def gates(r):
        gate, up = gu_acc[r, :h], gu_acc[r, h:]
        sig = 1.0 / (1.0 + jnp.exp(-gate))
        return gate, up, sig, gate * sig

    for j in range(rows // tile):
        r = pl.ds(j * tile, tile)
        gate, up, sig, silu = gates(r)
        hid_ref[r, :] = (silu * up).astype(BF16)
    for i in range(nz):
        wait_bytes(slots.at[0, pl.ds(0, rows - cap)], tpush_send.at[i])

    split = 128 * ((width // 128 + 1) // 2)
    parts = ((0, split), (split, width - split))
    owns = {}

    def down(u, sides=(0, 1)):
        for d in sides:
            o = at((-1 - u, 1 + u)[d])
            first, count = parts[d]
            cols, here = pl.ds(pl.multiple_of(o * width + first, 128), count), pl.ds(first, count)

            def body(j, _):
                r = pl.ds(pl.multiple_of(j * tile, tile), tile)
                slots[o, r, here] = jnp.dot(hid_ref[r, :], wd_ref[:, cols], preferred_element_type=F32).astype(BF16)
                return 0

            lax.fori_loop(0, rows // tile, body, 0)

            def push(j, _):
                q = lax.rem(me + j, nx)
                remote(
                    slots.at[o, slab(q), here], ret.at[o, slab(me), here],
                    push_send.at[d, u], push_recv.at[d, u], expert=q, tensor=t,
                ).start()
                return 0

            lax.fori_loop(1, nx, push, 0)
            own = pltpu.make_async_copy(slots.at[o, slab(me), here], ret.at[o, slab(me), here], self_sem.at[d, u])
            own.start()
            owns[d, u] = own

    down(0, (0,))
    cot_step(7)
    down(0, (1,))
    add_cot(7)
    for j in range(rows // tile):
        r = pl.ds(j * tile, tile)
        gate, up, sig, silu = gates(r)
        d_hidden = dh_acc[r, :]
        dgu_ref[r, :h] = (d_hidden * up * sig * (1.0 + gate * (1.0 - sig))).astype(BF16)
        dgu_ref[r, h:] = (d_hidden * silu).astype(BF16)
        dots = jnp.sum(hid_ref[r, :].astype(F32) * d_hidden, axis=1, keepdims=True)
        dsrc[r, :] = jnp.broadcast_to(dots, (tile, dsrc.shape[1]))

    def push_dots(i, _):
        q = lax.rem(me + i, nx)
        remote(dsrc.at[slab(q)], dret.at[slab(me)], d_send, d_recv, expert=q, tensor=t).start()
        return 0

    fill_bk(0, at(-1), rs0)
    fill_bk(1, at(1), rs0)
    for p in range(RS_PIECES):
        for d in range(2):
            go(rs_copy(0, d, p))
    down(1)
    lax.fori_loop(1, nx, push_dots, 0)
    dret[slab(me), :] = dsrc[slab(me), :]
    hid_t[...] = hid_ref[...].astype(F32).T.astype(BF16)
    dgu_t[...] = dgu_ref[...].astype(F32).T.astype(BF16)

    def load(o):
        return (
            pltpu.make_async_copy(routed_ref.at[o], routed_v.at[o % 2], load_sem.at[0, o % 2]),
            pltpu.make_async_copy(rcot_ref.at[o], rcot_v.at[o % 2], load_sem.at[1, o % 2]),
        )

    def store(o):
        r = pl.ds(o * width, width)
        return (
            pltpu.make_async_copy(ggu_v.at[o % 2, 0], gg_ref.at[r], store_sem.at[0, o % 2]),
            pltpu.make_async_copy(ggu_v.at[o % 2, 1], gu_ref.at[r], store_sem.at[1, o % 2]),
            pltpu.make_async_copy(gd_v.at[o % 2], gd_ref.at[:, r], store_sem.at[2, o % 2]),
        )

    for c in load(0):
        c.start()

    def grads(o):
        for c in load(o):
            c.wait()
        if o + 1 < nz:
            for c in load(o + 1):
                c.start()
        if o >= 2:
            for c in store(o - 2):
                c.wait()
        s = o % 2
        gd_v[s] = jnp.dot(hid_t[...], rcot_v[s], preferred_element_type=F32).astype(BF16)
        both = jnp.dot(dgu_t[...], routed_v[s], preferred_element_type=F32).T.astype(BF16)
        ggu_v[s, 0] = both[:, :h]
        ggu_v[s, 1] = both[:, h:]
        for c in store(o):
            c.start()

    def rs2_copy(k, d):
        cols = pl.ds(*parts[d])
        return remote(
            rs2_0.at[:, cols] if k == 0 else rs2.at[k - 1, :, cols], rs2.at[k, :, cols],
            rs2_send.at[d, k], rs2_recv.at[d, k], expert=me, tensor=(right, left)[d],
        )

    def rs2_step(u):
        for d in range(2):
            o, cols = at((-1 - u, 1 + u)[d]), pl.ds(*parts[d])
            owns[d, u].wait()
            wait_bytes(ret.at[0, pl.ds(0, rows - cap), cols], push_recv.at[d, u])
            chosen = jnp.dot(pick[...], ret[o, :, cols], preferred_element_type=F32)
            mix_v[:, cols] = w_col_ref[:, 0:1] * chosen[:n_tok] + w_col_ref[:, 1:2] * chosen[n_tok:]
        for d in range(2):
            cols = pl.ds(*parts[d])
            part = mix_v[:, cols]
            if u == 0:
                rs2_0[:, cols] = part.astype(BF16)
            else:
                rs2_copy(u - 1, d).wait_recv()
                part = rs2[u - 1, :, cols].astype(F32) + part
                if u < nz - 1:
                    rs2[u - 1, :, cols] = part.astype(BF16)
                else:
                    mixed_ref[:, cols] = part.astype(BF16)
            if u < nz - 1:
                go(rs2_copy(u, d))

    def route_part():
        wait_bytes(dret.at[pl.ds(0, rows - cap)], d_recv)
        j = lax.broadcasted_iota(jnp.int32, (rows, n_tok), 0).astype(F32)
        dpart[...] = jnp.zeros_like(dpart)
        for k, target in enumerate(row_targets):
            dpart[k : k + 1, :] = jnp.sum(jnp.where(j == target, dret[...], 0.0), axis=0, keepdims=True)

        def share(i, _):
            remote(dpart, dsum.at[t], z_send, z_recv, expert=me, tensor=lax.rem(t + i, nz)).start()
            return 0

        lax.fori_loop(1, nz, share, 0)
        dsum[t] = dpart[...]

    size = half // RS_PIECES
    for k in range(1, nz):
        for d in range(2):
            fill_bk(d, at((-1 - k, 1 + k)[d]), bk)
        if k + 1 < nz:
            down(k + 1)
        for p in range(RS_PIECES):
            r = pl.ds(p * size, size)
            for d in range(2):
                rs_copy(k - 1, d, p).wait_recv()
                total = (rs[d, k - 1, r, :].astype(F32) + bk[d, r, :]).astype(BF16)
                if k < nz - 1:
                    rs[d, k - 1, r, :] = total
                    go(rs_copy(k, d, p))
                    continue
                islots[pl.ds(d * half + p * size, size), :] = total
                first, count = (d * half + p * size) // cap, size // cap

                def push_grad(i, _):
                    q = first + lax.rem(me + i, count)

                    @pl.when(q != me)
                    def _():
                        remote(islots.at[slab(q)], gret.at[slab(me)], g_send, g_recv, expert=q, tensor=t).start()

                    return 0

                lax.fori_loop(0, count, push_grad, 0)
        grads(k - 1)
        if k == 2:
            route_part()
        if k >= RS2_LAG:
            rs2_step(k - RS2_LAG)
    gret[slab(me), :] = islots[slab(me), :]
    for u in range(nz - RS2_LAG, nz - 1):
        rs2_step(u)
        if u == nz - RS2_LAG:
            grads(nz - 1)
    wait_bytes(gret.at[pl.ds(0, rows - cap)], g_recv)
    chosen = jnp.dot(pick[...], gret[...], preferred_element_type=F32)
    gtok_ref[...] = (w_col_ref[:, 0:1] * chosen[:n_tok] + w_col_ref[:, 1:2] * chosen[n_tok:]).astype(BF16)
    rs2_step(nz - 1)

    wait_bytes(dsum.at[pl.ds(0, nz - 1)], z_recv)
    total = dsum[0]
    for z in range(1, nz):
        total = total + dsum[z]
    groute_ref[...] = total[0:2, :] / w_row_ref[...]

    for o in (nz - 2, nz - 1):
        for c in store(o):
            c.wait()
    for c in started:
        c.wait_send()
    for d in range(2):
        for u in range(nz):
            wait_bytes(ret.at[0, pl.ds(0, rows - cap), pl.ds(*parts[d])], push_send.at[d, u])
    wait_bytes(islots.at[pl.ds(0, rows - cap)], g_send)
    wait_bytes(dsrc.at[pl.ds(0, rows - cap)], d_send)
    wait_bytes(dsum.at[pl.ds(0, nz - 1)], z_send)
    wait_bytes(cslots.at[pl.ds(0, rows - cap)], cpush_send)


def layer(nx, nz, cap, ids_t, weights_t, tokens, cotangent, wg, wu, wd):
    n_tok, width = tokens.shape
    h = wg.shape[1]
    rows = nx * cap
    dma = pltpu.SemaphoreType.DMA
    small = jax.ShapeDtypeStruct((n_tok, width), BF16)
    tall = jax.ShapeDtypeStruct((nz * width, h), BF16)
    buffer = jax.ShapeDtypeStruct((nz, rows, width), BF16)
    return pl.pallas_call(
        functools.partial(layer_kernel, nx, nz, cap),
        out_shape=(
            buffer, buffer, small, small, jax.ShapeDtypeStruct((2, n_tok), F32), tall, tall,
            jax.ShapeDtypeStruct((h, nz * width), BF16),
        ),
        in_specs=[VMEM] * 4 + [ANY] * 3,
        out_specs=(ANY, ANY, VMEM, VMEM, VMEM, ANY, ANY, ANY),
        scratch_shapes=[
            pltpu.VMEM((nz * width, h), BF16),
            pltpu.VMEM((nz * width, h), BF16),
            pltpu.VMEM((h, nz * width), BF16),
            pltpu.VMEM((rows, n_tok), BF16),
            pltpu.VMEM((nz, n_tok, width), BF16),
            pltpu.VMEM((nz, rows, width), BF16),
            pltpu.VMEM((rows, width), BF16),
            pltpu.VMEM((rows, 2 * h), F32),
            pltpu.VMEM((rows, h), F32),
            pltpu.VMEM((rows, h), BF16),
            pltpu.VMEM((rows, 2 * h), BF16),
            pltpu.VMEM((n_tok, 2), F32),
            pltpu.VMEM((2 * n_tok, rows), BF16),
            pltpu.VMEM((h, rows), BF16),
            pltpu.VMEM((2 * h, rows), BF16),
            pltpu.VMEM((nz, rows, width), BF16),
            pltpu.VMEM((2, rows // 2, width), BF16),
            pltpu.VMEM((2, nz - 1, rows // 2, width), BF16),
            pltpu.VMEM((2, rows // 2, width), F32),
            pltpu.VMEM((rows, width), BF16),
            pltpu.VMEM((rows, width), BF16),
            pltpu.VMEM((n_tok, width), F32),
            pltpu.VMEM((n_tok, width), BF16),
            pltpu.VMEM((nz - 1, n_tok, width), BF16),
            pltpu.VMEM((rows, 128), F32),
            pltpu.VMEM((rows, 128), F32),
            pltpu.VMEM((8, n_tok), F32),
            pltpu.VMEM((nz, 8, n_tok), F32),
            pltpu.VMEM((2, rows, width), BF16),
            pltpu.VMEM((2, rows, width), BF16),
            pltpu.VMEM((2, 2, width, h), BF16),
            pltpu.VMEM((2, h, width), BF16),
            dma((2, nz // 2, PIECES)), dma((2, nz // 2, PIECES)), dma((nz,)), dma((nz,)), dma((nz,)), dma, dma, dma,
            dma((2, nz - 1, PIECES)), dma((2, nz - 1, PIECES)), dma((2, 2, PIECES)), dma((3,)),
            dma((2, nz)), dma((2, nz)), dma((2, nz)),
            dma((2, nz - 1, RS_PIECES)), dma((2, nz - 1, RS_PIECES)),
            dma, dma, dma((2, nz - 1)), dma((2, nz - 1)),
            dma, dma, dma, dma, dma((2, 2)), dma((3, 2)),
        ],
        compiler_params=pltpu.CompilerParams(
            collective_id=0, has_side_effects=True, vmem_limit_bytes=62 * 1024 * 1024
        ),
        name="layer",
    )(ids_t, weights_t, tokens, cotangent, wg, wu, wd)


CHUNKS = 4


def finish_kernel(*refs):
    n = 6
    ins, outs, held, get, put = refs[:n], refs[n : 2 * n], refs[2 * n : 3 * n], refs[3 * n], refs[3 * n + 1]

    def pieces():
        at = 0
        for a, (src, dst, v) in enumerate(zip(ins, outs, held)):
            axis = 0 if src.shape[0] >= src.shape[1] else 1
            size = src.shape[axis] // CHUNKS if max(src.shape) >= 1024 * CHUNKS else src.shape[axis]
            for c in range(src.shape[axis] // size):
                where = (pl.ds(c * size, size), slice(None)) if axis == 0 else (slice(None), pl.ds(c * size, size))
                yield (
                    pltpu.make_async_copy(src.at[where], v.at[where], get.at[at]),
                    pltpu.make_async_copy(v.at[where], dst.at[where], put.at[at]),
                )
                at += 1

    moves = list(pieces())
    for load, _ in moves:
        load.start()
    for load, store in moves:
        load.wait()
        store.start()
    for _, store in moves:
        store.wait()


def finish(*arrays):
    n = len(arrays)
    shapes = tuple(jax.ShapeDtypeStruct(a.shape, a.dtype) for a in arrays)
    return pl.pallas_call(
        finish_kernel,
        out_shape=shapes,
        in_specs=[ANY] * n,
        out_specs=(ANY,) * n,
        scratch_shapes=[pltpu.VMEM(a.shape, a.dtype) for a in arrays]
        + [pltpu.SemaphoreType.DMA((n * CHUNKS,)), pltpu.SemaphoreType.DMA((n * CHUNKS,))],
        compiler_params=pltpu.CompilerParams(vmem_limit_bytes=62 * 1024 * 1024),
        name="finish",
    )(*arrays)


def local(tokens, ids, weights, cotangent, w_gate, w_up, w_down):
    nx, nz = lax.axis_size("expert"), lax.axis_size("tensor")
    cap = 4 * tokens.shape[0] // nx
    results = layer(nx, nz, cap, ids.T, weights.T, tokens, cotangent, w_gate[0], w_up[0], w_down[0])
    mixed, grad_tokens, grad_route, grad_gate, grad_up, grad_down = finish(*results[2:])
    return (mixed, grad_tokens, grad_route.T, grad_gate[None], grad_up[None], grad_down[None])


def solution(mesh):
    placed = (
        P("expert", "tensor"),
        P("expert", None),
        P("expert", None),
        P("expert", "tensor"),
        P("expert", None, "tensor"),
        P("expert", None, "tensor"),
        P("expert", "tensor", None),
    )
    return jax.shard_map(
        local,
        mesh=mesh,
        in_specs=placed,
        out_specs=(
            P("expert", "tensor"),
            P("expert", "tensor"),
            P("expert", None),
            P("expert", None, "tensor"),
            P("expert", None, "tensor"),
            P("expert", "tensor", None),
        ),
        check_vma=False,
    )
```

```python
import functools

import jax
import jax.numpy as jnp
from jax import lax
from jax.experimental import pallas as pl
from jax.experimental.pallas import tpu as pltpu
from jax.sharding import PartitionSpec as P

MESH = pl.DeviceIdType.MESH
F32 = jnp.float32
BF16 = jnp.bfloat16
NT_DIMS = (((1,), (1,)), ((), ()))
VMEM = pl.BlockSpec(memory_space=pltpu.VMEM)
ANY = pl.BlockSpec(memory_space=pl.ANY)


def remote(src, dst, send, recv, **where):
    return pltpu.make_async_remote_copy(
        src_ref=src, dst_ref=dst, send_sem=send, recv_sem=recv, device_id=where, device_id_type=MESH
    )


def wait_bytes(ref, sem):
    pltpu.make_async_copy(ref, ref, sem).wait()


def columns_of(row):
    n = row.shape[1]
    return jnp.broadcast_to(row, (n, n)).T


def slot_targets(rows, cols, cap, axis):
    n = rows[0].shape[1]
    here = lax.broadcasted_iota(jnp.int32, (n, n), 1 - axis)
    there = lax.broadcasted_iota(jnp.int32, (n, n), axis)
    targets = []
    for k in range(2):
        mine, others = (rows, cols) if axis == 0 else (cols, rows)
        count = None
        for other in range(2):
            before = there <= here if other < k else there < here
            hit = (others[other] == mine[k]) & before
            seen = jnp.sum(jnp.where(hit, 1.0, 0.0), axis=axis, keepdims=True)
            count = seen if count is None else count + seen
        own = mine[k] if axis == 0 else mine[k][:, 0:1]
        targets.append(own * cap + count)
    return targets


PIECES = 2
RS_PIECES = 2
RS2_LAG = 3


def layer_kernel(
    nx, nz, cap,
    ids_ref, w_row_ref, tok_ref, cot_ref, wg_hbm, wu_hbm, wd_hbm,
    routed_ref, rcot_ref, mixed_ref, gtok_ref, groute_ref, gg_ref, gu_ref, gd_ref,
    wg_ref, wu_ref, wd_ref, sel_ref, tokbuf, slots, cslots, gu_acc, dh_acc, hid_ref, dgu_ref, w_col_ref,
    pick, hid_t, dgu_t, ret, rs0, rs, bk, islots, gret, mix_v, rs2_0, rs2, dsrc, dret, dpart, dsum,
    routed_v, rcot_v,
    ring_send, ring_recv, tpush_send, tpush_recv, tself_sem, cpush_send, cpush_recv, cself_sem,
    cring_send, cring_recv, cload_sem, weight_sem,
    push_send, push_recv, self_sem, rs_send, rs_recv, g_send, g_recv, rs2_send, rs2_recv,
    d_send, d_recv, z_send, z_recv, load_sem,
):
    me, t = lax.axis_index("expert"), lax.axis_index("tensor")
    n_tok, width = tok_ref.shape
    rows, h = hid_ref.shape
    half, thalf = rows // 2, n_tok // 2
    right, left = lax.rem(t + 1, nz), lax.rem(t + nz - 1, nz)
    tile = 128
    barrier = pltpu.get_barrier_semaphore()

    def hello(i, _):
        pl.semaphore_signal(
            barrier, inc=1, device_id={"expert": lax.rem(me + i, nx), "tensor": t}, device_id_type=MESH
        )
        return 0

    def hello_z(i, _):
        pl.semaphore_signal(
            barrier, inc=1, device_id={"expert": me, "tensor": lax.rem(t + i, nz)}, device_id_type=MESH
        )
        return 0

    lax.fori_loop(1, nx, hello, 0)
    lax.fori_loop(1, nz, hello_z, 0)
    weight_loads = [
        pltpu.make_async_copy(src, dst, weight_sem.at[i])
        for i, (src, dst) in enumerate(((wg_hbm, wg_ref), (wu_hbm, wu_ref), (wd_hbm, wd_ref)))
    ]
    for c in weight_loads:
        c.start()

    def slab(e):
        return pl.ds(pl.multiple_of(e * cap, cap), cap)

    def at(step):
        return lax.rem(t + 2 * nz + step, nz)

    started = []

    def go(c):
        c.start()
        started.append(c)

    id_rows = [ids_ref[k : k + 1, :].astype(F32) for k in range(2)]
    id_cols = [columns_of(r) for r in id_rows]
    row_targets = slot_targets(id_rows, id_cols, cap, 0)
    w0, w1 = w_row_ref[0:1, :], w_row_ref[1:2, :]
    for k in range(2):
        w_col_ref[:, k : k + 1] = columns_of(w_row_ref[k : k + 1, :])[:, 0:1]

    def select(i, _):
        r = pl.ds(pl.multiple_of(i * tile, tile), tile)
        j = (lax.broadcasted_iota(jnp.int32, (tile, n_tok), 0) + i * tile).astype(F32)
        hit0, hit1 = j == row_targets[0], j == row_targets[1]
        sel = jnp.where(hit0 | hit1, 1.0, 0.0).astype(BF16)
        sel_ref[r, :] = sel
        w = jnp.sum(jnp.where(hit0, w0, 0.0) + jnp.where(hit1, w1, 0.0), axis=1, keepdims=True)
        cslots[r, :] = (w * jnp.dot(sel, cot_ref[...], preferred_element_type=F32)).astype(BF16)
        return 0

    lax.fori_loop(0, rows // tile, select, 0)

    def fill(o, block):
        def body(i, _):
            r = pl.ds(pl.multiple_of(i * tile, tile), tile)
            slots[o, r, :] = jnp.dot(sel_ref[r, :], block[...], preferred_element_type=F32).astype(BF16)
            return 0

        lax.fori_loop(0, rows // tile, body, 0)

    fill(t, tok_ref)
    pl.semaphore_wait(barrier, nx + nz - 2)

    def ring(d, k, p):
        o, size = at((-k, k)[d]), n_tok // PIECES
        r = pl.ds(p * size, size)
        return remote(
            tok_ref.at[r] if k == 0 else tokbuf.at[o, r], tokbuf.at[o, r],
            ring_send.at[d, k, p], ring_recv.at[d, k, p], expert=me, tensor=(right, left)[d],
        )

    ring_hops = (nz // 2, nz - 1 - nz // 2)
    for p in range(PIECES):
        for d in range(2):
            go(ring(d, 0, p))

    def push_cot(i, _):
        q = lax.rem(me + i, nx)
        remote(cslots.at[slab(q)], rcot_ref.at[t, slab(me)], cpush_send, cpush_recv, expert=q, tensor=t).start()
        return 0

    lax.fori_loop(1, nx, push_cot, 0)
    own_cot = pltpu.make_async_copy(cslots.at[slab(me)], rcot_ref.at[t, slab(me)], cself_sem)
    own_cot.start()
    token_order, token_owns = [], []

    def push_tok(step):
        i, o = len(token_order), at(step)

        def body(j, _):
            q = lax.rem(me + j, nx)
            remote(
                slots.at[o, slab(q)], routed_ref.at[o, slab(me)], tpush_send.at[i], tpush_recv.at[i],
                expert=q, tensor=t,
            ).start()
            return 0

        lax.fori_loop(1, nx, body, 0)
        own = pltpu.make_async_copy(slots.at[o, slab(me)], routed_ref.at[o, slab(me)], tself_sem.at[i])
        own.start()
        token_owns.append(own)
        token_order.append(step)

    def cot_ring(d, k, p):
        o, size = at((-k, k)[d]), half // PIECES
        r = pl.ds(d * half + p * size, size)
        return remote(
            rcot_ref.at[o, r], rcot_ref.at[o, r], cring_send.at[d, k, p], cring_recv.at[d, k, p],
            expert=me, tensor=(right, left)[d],
        )

    def token_step(k):
        came = [d for d in range(2) if k <= ring_hops[d]]
        for p in range(PIECES):
            for d in came:
                ring(d, k - 1, p).wait_recv()
                if k < ring_hops[d]:
                    go(ring(d, k, p))
        for d in came:
            step = (-k, k)[d]
            fill(at(step), tokbuf.at[at(step)])
            push_tok(step)

    def cot_load(d, k, p):
        size = half // PIECES
        r = pl.ds(d * half + p * size, size)
        return pltpu.make_async_copy(
            rcot_ref.at[at((-k, k)[d]), r], rcot_v.at[k % 2, r], cload_sem.at[d, k % 2, p]
        )

    def cot_step(k):
        for p in range(PIECES):
            for d in range(2):
                if k > 0:
                    cot_ring(d, k - 1, p).wait_recv()
                if k < nz - 1:
                    go(cot_ring(d, k, p))
                cot_load(d, k, p).start()

    def add_cot(k):
        for d in range(2):
            r = pl.ds(d * half, half)
            for p in range(PIECES):
                cot_load(d, k, p).wait()
            cols = pl.ds(pl.multiple_of(at((-k, k)[d]) * width, 128), width)
            dh = lax.dot_general(rcot_v[k % 2, r, :], wd_ref[:, cols], NT_DIMS, preferred_element_type=F32)
            dh_acc[r, :] = dh if k == 0 else dh_acc[r, :] + dh

    def tok_load(i):
        return pltpu.make_async_copy(routed_ref.at[at(token_order[i])], routed_v.at[i % 2], tself_sem.at[i])

    def start_tok(i):
        token_owns[i].wait()
        wait_bytes(slots.at[0, pl.ds(0, rows - cap)], tpush_recv.at[i])
        tok_load(i).start()

    def add_tok(i):
        tok_load(i).wait()
        w = weight_block(at(token_order[i]))
        for j in range(rows // tile):
            r = pl.ds(j * tile, tile)
            gu = jnp.dot(routed_v[i % 2, r, :], w, preferred_element_type=F32)
            gu_acc[r, :] = gu if i == 0 else gu_acc[r, :] + gu

    def weight_block(o):
        r = pl.ds(pl.multiple_of(o * width, 128), width)
        return jnp.concatenate([wg_ref[r, :], wu_ref[r, :]], axis=1)

    def fill_bk(d, o, into):
        w = weight_block(o)
        for i in range(half // tile):
            lhs = dgu_ref[pl.ds(d * half + i * tile, tile), :]
            into[d, pl.ds(i * tile, tile), :] = lax.dot_general(
                lhs, w, NT_DIMS, preferred_element_type=F32
            ).astype(into.dtype)

    def rs_copy(k, d, p):
        size = half // RS_PIECES
        r = pl.ds(p * size, size)
        return remote(
            rs0.at[d, r] if k == 0 else rs.at[d, k - 1, r], rs.at[d, k, r],
            rs_send.at[d, k, p], rs_recv.at[d, k, p], expert=me, tensor=(right, left)[d],
        )

    push_tok(0)
    token_step(1)
    wait_bytes(cslots.at[pl.ds(0, rows - cap)], cpush_recv)
    own_cot.wait()
    cot_step(0)
    token_step(2)
    cot_step(1)
    for c in weight_loads:
        c.wait()
    add_cot(0)
    token_step(3)
    cot_step(2)
    add_cot(1)
    token_step(4)
    cot_step(3)
    start_tok(0)
    add_cot(2)
    start_tok(1)
    add_tok(0)
    cot_step(4)
    start_tok(2)
    add_cot(3)
    add_tok(1)
    start_tok(3)
    add_tok(2)
    cot_step(5)
    start_tok(4)
    add_cot(4)
    add_tok(3)
    start_tok(5)
    add_tok(4)
    cot_step(6)
    start_tok(6)
    add_cot(5)
    add_tok(5)
    add_tok(6)
    add_cot(6)
    lanes = lax.broadcasted_iota(jnp.int32, (n_tok, rows), 1).astype(F32)
    for k, target in enumerate(slot_targets(id_rows, id_cols, cap, 1)):
        pick[pl.ds(k * n_tok, n_tok), :] = jnp.where(lanes == target, 1.0, 0.0).astype(BF16)
    start_tok(7)
    add_tok(7)

    def gates(r):
        gate, up = gu_acc[r, :h], gu_acc[r, h:]
        sig = 1.0 / (1.0 + jnp.exp(-gate))
        return gate, up, sig, gate * sig

    for j in range(rows // tile):
        r = pl.ds(j * tile, tile)
        gate, up, sig, silu = gates(r)
        hid_ref[r, :] = (silu * up).astype(BF16)
    for i in range(nz):
        wait_bytes(slots.at[0, pl.ds(0, rows - cap)], tpush_send.at[i])

    split = 128 * ((width // 128 + 1) // 2)
    parts = ((0, split), (split, width - split))
    owns = {}

    def down(u, sides=(0, 1)):
        for d in sides:
            o = at((-1 - u, 1 + u)[d])
            first, count = parts[d]
            cols, here = pl.ds(pl.multiple_of(o * width + first, 128), count), pl.ds(first, count)

            def body(j, _):
                r = pl.ds(pl.multiple_of(j * tile, tile), tile)
                slots[o, r, here] = jnp.dot(hid_ref[r, :], wd_ref[:, cols], preferred_element_type=F32).astype(BF16)
                return 0

            lax.fori_loop(0, rows // tile, body, 0)

            def push(j, _):
                q = lax.rem(me + j, nx)
                remote(
                    slots.at[o, slab(q), here], ret.at[o, slab(me), here],
                    push_send.at[d, u], push_recv.at[d, u], expert=q, tensor=t,
                ).start()
                return 0

            lax.fori_loop(1, nx, push, 0)
            own = pltpu.make_async_copy(slots.at[o, slab(me), here], ret.at[o, slab(me), here], self_sem.at[d, u])
            own.start()
            owns[d, u] = own

    down(0, (0,))
    cot_step(7)
    down(0, (1,))
    add_cot(7)
    for j in range(rows // tile):
        r = pl.ds(j * tile, tile)
        gate, up, sig, silu = gates(r)
        d_hidden = dh_acc[r, :]
        dgu_ref[r, :h] = (d_hidden * up * sig * (1.0 + gate * (1.0 - sig))).astype(BF16)
        dgu_ref[r, h:] = (d_hidden * silu).astype(BF16)
        dots = jnp.sum(hid_ref[r, :].astype(F32) * d_hidden, axis=1, keepdims=True)
        dsrc[r, :] = jnp.broadcast_to(dots, (tile, dsrc.shape[1]))

    def push_dots(i, _):
        q = lax.rem(me + i, nx)
        remote(dsrc.at[slab(q)], dret.at[slab(me)], d_send, d_recv, expert=q, tensor=t).start()
        return 0

    fill_bk(0, at(-1), rs0)
    fill_bk(1, at(1), rs0)
    for p in range(RS_PIECES):
        for d in range(2):
            go(rs_copy(0, d, p))
    down(1)
    lax.fori_loop(1, nx, push_dots, 0)
    dret[slab(me), :] = dsrc[slab(me), :]
    hid_t[...] = hid_ref[...].astype(F32).T.astype(BF16)
    dgu_t[...] = dgu_ref[...].astype(F32).T.astype(BF16)

    def load(o):
        return (
            pltpu.make_async_copy(routed_ref.at[o], routed_v.at[o % 2], load_sem.at[0, o % 2]),
            pltpu.make_async_copy(rcot_ref.at[o], rcot_v.at[o % 2], load_sem.at[1, o % 2]),
        )

    for c in load(0):
        c.start()

    def grads(o):
        for c in load(o):
            c.wait()
        if o + 1 < nz:
            for c in load(o + 1):
                c.start()
        s = o % 2
        r = pl.ds(o * width, width)
        gd_ref[:, r] = jnp.dot(hid_t[...], rcot_v[s], preferred_element_type=F32).astype(BF16)
        both = jnp.dot(dgu_t[...], routed_v[s], preferred_element_type=F32).T.astype(BF16)
        gg_ref[r, :] = both[:, :h]
        gu_ref[r, :] = both[:, h:]

    def rs2_copy(k, d, p):
        cols, size = pl.ds(*parts[d]), n_tok // RS_PIECES
        r = pl.ds(p * size, size)
        return remote(
            rs2_0.at[r, cols] if k == 0 else rs2.at[k - 1, r, cols], rs2.at[k, r, cols],
            rs2_send.at[d, k, p], rs2_recv.at[d, k, p], expert=me, tensor=(right, left)[d],
        )

    def rs2_step(u):
        for d in range(2):
            o, cols = at((-1 - u, 1 + u)[d]), pl.ds(*parts[d])
            owns[d, u].wait()
            wait_bytes(ret.at[0, pl.ds(0, rows - cap), cols], push_recv.at[d, u])
            chosen = jnp.dot(pick[...], ret[o, :, cols], preferred_element_type=F32)
            mix_v[:, cols] = w_col_ref[:, 0:1] * chosen[:n_tok] + w_col_ref[:, 1:2] * chosen[n_tok:]
        for p in range(RS_PIECES):
            r = pl.ds(p * (n_tok // RS_PIECES), n_tok // RS_PIECES)
            for d in range(2):
                cols = pl.ds(*parts[d])
                part = mix_v[r, cols]
                if u == 0:
                    rs2_0[r, cols] = part.astype(BF16)
                else:
                    rs2_copy(u - 1, d, p).wait_recv()
                    part = rs2[u - 1, r, cols].astype(F32) + part
                    if u < nz - 1:
                        rs2[u - 1, r, cols] = part.astype(BF16)
                    else:
                        mixed_ref[r, cols] = part.astype(BF16)
                if u < nz - 1:
                    go(rs2_copy(u, d, p))

    def route_part():
        wait_bytes(dret.at[pl.ds(0, rows - cap)], d_recv)
        j = lax.broadcasted_iota(jnp.int32, (rows, n_tok), 0).astype(F32)
        dpart[...] = jnp.zeros_like(dpart)
        for k, target in enumerate(row_targets):
            dpart[k : k + 1, :] = jnp.sum(jnp.where(j == target, dret[...], 0.0), axis=0, keepdims=True)

        def share(i, _):
            remote(dpart, dsum.at[t], z_send, z_recv, expert=me, tensor=lax.rem(t + i, nz)).start()
            return 0

        lax.fori_loop(1, nz, share, 0)
        dsum[t] = dpart[...]

    size = half // RS_PIECES
    for k in range(1, nz):
        for d in range(2):
            fill_bk(d, at((-1 - k, 1 + k)[d]), bk)
        if k + 1 < nz:
            down(k + 1)
        for p in range(RS_PIECES):
            r = pl.ds(p * size, size)
            for d in range(2):
                rs_copy(k - 1, d, p).wait_recv()
                total = (rs[d, k - 1, r, :].astype(F32) + bk[d, r, :]).astype(BF16)
                if k < nz - 1:
                    rs[d, k - 1, r, :] = total
                    go(rs_copy(k, d, p))
                    continue
                islots[pl.ds(d * half + p * size, size), :] = total
                first, count = (d * half + p * size) // cap, size // cap

                def push_grad(i, _):
                    q = first + lax.rem(me + i, count)

                    @pl.when(q != me)
                    def _():
                        remote(islots.at[slab(q)], gret.at[slab(me)], g_send, g_recv, expert=q, tensor=t).start()

                    return 0

                lax.fori_loop(0, count, push_grad, 0)
        if k <= 2:
            grads(k - 1)
        if k >= 2:
            grads(k)
        if k == 4:
            route_part()
        if k >= RS2_LAG:
            rs2_step(k - RS2_LAG)
    gret[slab(me), :] = islots[slab(me), :]
    for u in range(nz - RS2_LAG, nz - 1):
        rs2_step(u)
    wait_bytes(gret.at[pl.ds(0, rows - cap)], g_recv)
    chosen = jnp.dot(pick[...], gret[...], preferred_element_type=F32)
    gtok_ref[...] = (w_col_ref[:, 0:1] * chosen[:n_tok] + w_col_ref[:, 1:2] * chosen[n_tok:]).astype(BF16)
    rs2_step(nz - 1)

    wait_bytes(dsum.at[pl.ds(0, nz - 1)], z_recv)
    total = dsum[0]
    for z in range(1, nz):
        total = total + dsum[z]
    groute_ref[...] = total[0:2, :] / w_row_ref[...]

    for c in started:
        c.wait_send()
    for d in range(2):
        for u in range(nz):
            wait_bytes(ret.at[0, pl.ds(0, rows - cap), pl.ds(*parts[d])], push_send.at[d, u])
    wait_bytes(islots.at[pl.ds(0, rows - cap)], g_send)
    wait_bytes(dsrc.at[pl.ds(0, rows - cap)], d_send)
    wait_bytes(dsum.at[pl.ds(0, nz - 1)], z_send)
    wait_bytes(cslots.at[pl.ds(0, rows - cap)], cpush_send)


def layer(nx, nz, cap, ids_t, weights_t, tokens, cotangent, wg, wu, wd):
    n_tok, width = tokens.shape
    h = wg.shape[1]
    rows = nx * cap
    dma = pltpu.SemaphoreType.DMA
    small = pltpu.VMEM((n_tok, width), BF16)
    tall = pltpu.VMEM((nz * width, h), BF16)
    buffer = jax.ShapeDtypeStruct((nz, rows, width), BF16)
    return pl.pallas_call(
        functools.partial(layer_kernel, nx, nz, cap),
        out_shape=(
            buffer, buffer, small, small, pltpu.VMEM((2, n_tok), F32), tall, tall,
            pltpu.VMEM((h, nz * width), BF16),
        ),
        in_specs=[VMEM] * 4 + [ANY] * 3,
        out_specs=(ANY, ANY, VMEM, VMEM, VMEM, VMEM, VMEM, VMEM),
        scratch_shapes=[
            pltpu.VMEM((nz * width, h), BF16),
            pltpu.VMEM((nz * width, h), BF16),
            pltpu.VMEM((h, nz * width), BF16),
            pltpu.VMEM((rows, n_tok), BF16),
            pltpu.VMEM((nz, n_tok, width), BF16),
            pltpu.VMEM((nz, rows, width), BF16),
            pltpu.VMEM((rows, width), BF16),
            pltpu.VMEM((rows, 2 * h), F32),
            pltpu.VMEM((rows, h), F32),
            pltpu.VMEM((rows, h), BF16),
            pltpu.VMEM((rows, 2 * h), BF16),
            pltpu.VMEM((n_tok, 2), F32),
            pltpu.VMEM((2 * n_tok, rows), BF16),
            pltpu.VMEM((h, rows), BF16),
            pltpu.VMEM((2 * h, rows), BF16),
            pltpu.VMEM((nz, rows, width), BF16),
            pltpu.VMEM((2, rows // 2, width), BF16),
            pltpu.VMEM((2, nz - 1, rows // 2, width), BF16),
            pltpu.VMEM((2, rows // 2, width), F32),
            pltpu.VMEM((rows, width), BF16),
            pltpu.VMEM((rows, width), BF16),
            pltpu.VMEM((n_tok, width), F32),
            pltpu.VMEM((n_tok, width), BF16),
            pltpu.VMEM((nz - 1, n_tok, width), BF16),
            pltpu.VMEM((rows, 128), F32),
            pltpu.VMEM((rows, 128), F32),
            pltpu.VMEM((8, n_tok), F32),
            pltpu.VMEM((nz, 8, n_tok), F32),
            pltpu.VMEM((2, rows, width), BF16),
            pltpu.VMEM((2, rows, width), BF16),
            dma((2, nz // 2, PIECES)), dma((2, nz // 2, PIECES)), dma((nz,)), dma((nz,)), dma((nz,)), dma, dma, dma,
            dma((2, nz - 1, PIECES)), dma((2, nz - 1, PIECES)), dma((2, 2, PIECES)), dma((3,)),
            dma((2, nz)), dma((2, nz)), dma((2, nz)),
            dma((2, nz - 1, RS_PIECES)), dma((2, nz - 1, RS_PIECES)),
            dma, dma, dma((2, nz - 1, RS_PIECES)), dma((2, nz - 1, RS_PIECES)),
            dma, dma, dma, dma, dma((2, 2)),
        ],
        compiler_params=pltpu.CompilerParams(
            collective_id=0, has_side_effects=True, vmem_limit_bytes=52 * 1024 * 1024
        ),
        name="layer",
    )(ids_t, weights_t, tokens, cotangent, wg, wu, wd)


CHUNKS = 4


def finish_kernel(*refs):
    n = 6
    ins, outs, put = refs[:n], refs[n : 2 * n], refs[2 * n]
    moves = []
    for src, dst in zip(ins, outs):
        axis = 0 if src.shape[0] >= src.shape[1] else 1
        count = CHUNKS if max(src.shape) >= 1024 * CHUNKS else 1
        size = src.shape[axis] // count
        for c in range(count):
            where = (pl.ds(c * size, size), slice(None)) if axis == 0 else (slice(None), pl.ds(c * size, size))
            moves.append(pltpu.make_async_copy(src.at[where], dst.at[where], put.at[len(moves)]))
    for move in moves:
        move.start()
    for move in moves:
        move.wait()


def finish(*arrays):
    n = len(arrays)
    shapes = tuple(jax.ShapeDtypeStruct(a.shape, a.dtype) for a in arrays)
    return pl.pallas_call(
        finish_kernel,
        out_shape=shapes,
        in_specs=[VMEM] * n,
        out_specs=(ANY,) * n,
        scratch_shapes=[pltpu.SemaphoreType.DMA((n * CHUNKS,))],
        compiler_params=pltpu.CompilerParams(vmem_limit_bytes=16 * 1024 * 1024),
        name="finish",
    )(*arrays)


def local(tokens, ids, weights, cotangent, w_gate, w_up, w_down):
    nx, nz = lax.axis_size("expert"), lax.axis_size("tensor")
    cap = 4 * tokens.shape[0] // nx
    results = layer(nx, nz, cap, ids.T, weights.T, tokens, cotangent, w_gate[0], w_up[0], w_down[0])
    mixed, grad_tokens, grad_route, grad_gate, grad_up, grad_down = finish(*results[2:])
    return (mixed, grad_tokens, grad_route.T, grad_gate[None], grad_up[None], grad_down[None])


def solution(mesh):
    placed = (
        P("expert", "tensor"),
        P("expert", None),
        P("expert", None),
        P("expert", "tensor"),
        P("expert", None, "tensor"),
        P("expert", None, "tensor"),
        P("expert", "tensor", None),
    )
    return jax.shard_map(
        local,
        mesh=mesh,
        in_specs=placed,
        out_specs=(
            P("expert", "tensor"),
            P("expert", "tensor"),
            P("expert", None),
            P("expert", None, "tensor"),
            P("expert", None, "tensor"),
            P("expert", "tensor", None),
        ),
        check_vma=False,
    )
```

```python
import functools

import jax
import jax.numpy as jnp
from jax import lax
from jax.experimental import pallas as pl
from jax.experimental.pallas import tpu as pltpu
from jax.sharding import PartitionSpec as P

MESH = pl.DeviceIdType.MESH
F32 = jnp.float32
BF16 = jnp.bfloat16
NT_DIMS = (((1,), (1,)), ((), ()))
VMEM = pl.BlockSpec(memory_space=pltpu.VMEM)
ANY = pl.BlockSpec(memory_space=pl.ANY)


def remote(src, dst, send, recv, **where):
    return pltpu.make_async_remote_copy(
        src_ref=src, dst_ref=dst, send_sem=send, recv_sem=recv, device_id=where, device_id_type=MESH
    )


def wait_bytes(ref, sem):
    pltpu.make_async_copy(ref, ref, sem).wait()


def columns_of(row):
    n = row.shape[1]
    return jnp.broadcast_to(row, (n, n)).T


def slot_targets(rows, cols, cap, axis):
    n = rows[0].shape[1]
    here = lax.broadcasted_iota(jnp.int32, (n, n), 1 - axis)
    there = lax.broadcasted_iota(jnp.int32, (n, n), axis)
    targets = []
    for k in range(2):
        mine, others = (rows, cols) if axis == 0 else (cols, rows)
        count = None
        for other in range(2):
            before = there <= here if other < k else there < here
            hit = (others[other] == mine[k]) & before
            seen = jnp.sum(jnp.where(hit, 1.0, 0.0), axis=axis, keepdims=True)
            count = seen if count is None else count + seen
        own = mine[k] if axis == 0 else mine[k][:, 0:1]
        targets.append(own * cap + count)
    return targets


PIECES = 2
RS_PIECES = 2
RS2_LAG = 3


def layer_kernel(
    nx, nz, cap,
    ids_ref, w_row_ref, tok_ref, cot_ref, wg_hbm, wu_hbm, wd_hbm,
    routed_ref, rcot_ref, mixed_ref, gtok_ref, groute_ref, gg_ref, gu_ref, gd_ref,
    wg_ref, wu_ref, wd_ref, sel_ref, tokbuf, slots, cslots, gu_acc, dh_acc, hid_ref, dgu_ref, w_col_ref,
    pick, hid_t, dgu_t, ret, rs0, rs, bk, islots, gret, mix_v, rs2_0, rs2, dsrc, dret, dpart, dsum,
    routed_v, rcot_v,
    ring_send, ring_recv, tpush_send, tpush_recv, tself_sem, cpush_send, cpush_recv, cself_sem,
    cring_send, cring_recv, cload_sem, weight_sem,
    push_send, push_recv, self_sem, rs_send, rs_recv, g_send, g_recv, rs2_send, rs2_recv,
    d_send, d_recv, z_send, z_recv, load_sem,
):
    me, t = lax.axis_index("expert"), lax.axis_index("tensor")
    n_tok, width = tok_ref.shape
    rows, h = hid_ref.shape
    half, thalf = rows // 2, n_tok // 2
    right, left = lax.rem(t + 1, nz), lax.rem(t + nz - 1, nz)
    tile = 128
    barrier = pltpu.get_barrier_semaphore()

    def hello(i, _):
        pl.semaphore_signal(
            barrier, inc=1, device_id={"expert": lax.rem(me + i, nx), "tensor": t}, device_id_type=MESH
        )
        return 0

    def hello_z(i, _):
        pl.semaphore_signal(
            barrier, inc=1, device_id={"expert": me, "tensor": lax.rem(t + i, nz)}, device_id_type=MESH
        )
        return 0

    lax.fori_loop(1, nx, hello, 0)
    lax.fori_loop(1, nz, hello_z, 0)
    weight_loads = [
        pltpu.make_async_copy(src, dst, weight_sem.at[i])
        for i, (src, dst) in enumerate(((wg_hbm, wg_ref), (wu_hbm, wu_ref), (wd_hbm, wd_ref)))
    ]
    for c in weight_loads:
        c.start()

    def slab(e):
        return pl.ds(pl.multiple_of(e * cap, cap), cap)

    def at(step):
        return lax.rem(t + 2 * nz + step, nz)

    started = []

    def go(c):
        c.start()
        started.append(c)

    id_rows = [ids_ref[k : k + 1, :].astype(F32) for k in range(2)]
    id_cols = [columns_of(r) for r in id_rows]
    row_targets = slot_targets(id_rows, id_cols, cap, 0)
    w0, w1 = w_row_ref[0:1, :], w_row_ref[1:2, :]
    for k in range(2):
        w_col_ref[:, k : k + 1] = columns_of(w_row_ref[k : k + 1, :])[:, 0:1]

    def select(i, _):
        r = pl.ds(pl.multiple_of(i * tile, tile), tile)
        j = (lax.broadcasted_iota(jnp.int32, (tile, n_tok), 0) + i * tile).astype(F32)
        hit0, hit1 = j == row_targets[0], j == row_targets[1]
        sel = jnp.where(hit0 | hit1, 1.0, 0.0).astype(BF16)
        sel_ref[r, :] = sel
        w = jnp.sum(jnp.where(hit0, w0, 0.0) + jnp.where(hit1, w1, 0.0), axis=1, keepdims=True)
        cslots[r, :] = (w * jnp.dot(sel, cot_ref[...], preferred_element_type=F32)).astype(BF16)
        return 0

    lax.fori_loop(0, rows // tile, select, 0)

    def fill(o, block):
        def body(i, _):
            r = pl.ds(pl.multiple_of(i * tile, tile), tile)
            slots[o, r, :] = jnp.dot(sel_ref[r, :], block[...], preferred_element_type=F32).astype(BF16)
            return 0

        lax.fori_loop(0, rows // tile, body, 0)

    fill(t, tok_ref)
    pl.semaphore_wait(barrier, nx + nz - 2)

    def ring(d, k, p):
        o, size = at((-k, k)[d]), n_tok // PIECES
        r = pl.ds(p * size, size)
        return remote(
            tok_ref.at[r] if k == 0 else tokbuf.at[o, r], tokbuf.at[o, r],
            ring_send.at[d, k, p], ring_recv.at[d, k, p], expert=me, tensor=(right, left)[d],
        )

    ring_hops = (nz // 2, nz - 1 - nz // 2)
    for p in range(PIECES):
        for d in range(2):
            go(ring(d, 0, p))

    def push_cot(i, _):
        q = lax.rem(me + i, nx)
        remote(cslots.at[slab(q)], rcot_ref.at[t, slab(me)], cpush_send, cpush_recv, expert=q, tensor=t).start()
        return 0

    lax.fori_loop(1, nx, push_cot, 0)
    own_cot = pltpu.make_async_copy(cslots.at[slab(me)], rcot_ref.at[t, slab(me)], cself_sem)
    own_cot.start()
    token_order, token_owns = [], []

    def push_tok(step):
        i, o = len(token_order), at(step)

        def body(j, _):
            q = lax.rem(me + j, nx)
            remote(
                slots.at[o, slab(q)], routed_ref.at[o, slab(me)], tpush_send.at[i], tpush_recv.at[i],
                expert=q, tensor=t,
            ).start()
            return 0

        lax.fori_loop(1, nx, body, 0)
        own = pltpu.make_async_copy(slots.at[o, slab(me)], routed_ref.at[o, slab(me)], tself_sem.at[i])
        own.start()
        token_owns.append(own)
        token_order.append(step)

    def cot_ring(d, k, p):
        o, size = at((-k, k)[d]), half // PIECES
        r = pl.ds(d * half + p * size, size)
        return remote(
            rcot_ref.at[o, r], rcot_ref.at[o, r], cring_send.at[d, k, p], cring_recv.at[d, k, p],
            expert=me, tensor=(right, left)[d],
        )

    def token_step(k):
        came = [d for d in range(2) if k <= ring_hops[d]]
        for p in range(PIECES):
            for d in came:
                ring(d, k - 1, p).wait_recv()
                if k < ring_hops[d]:
                    go(ring(d, k, p))
        for d in came:
            step = (-k, k)[d]
            fill(at(step), tokbuf.at[at(step)])
            push_tok(step)

    def cot_load(d, k, p):
        size = half // PIECES
        r = pl.ds(d * half + p * size, size)
        return pltpu.make_async_copy(
            rcot_ref.at[at((-k, k)[d]), r], rcot_v.at[k % 2, r], cload_sem.at[d, k % 2, p]
        )

    def cot_step(k):
        for p in range(PIECES):
            for d in range(2):
                if k > 0:
                    cot_ring(d, k - 1, p).wait_recv()
                if k < nz - 1:
                    go(cot_ring(d, k, p))
                cot_load(d, k, p).start()

    def add_cot(k):
        for d in range(2):
            r = pl.ds(d * half, half)
            for p in range(PIECES):
                cot_load(d, k, p).wait()
            cols = pl.ds(pl.multiple_of(at((-k, k)[d]) * width, 128), width)
            dh = lax.dot_general(rcot_v[k % 2, r, :], wd_ref[:, cols], NT_DIMS, preferred_element_type=F32)
            dh_acc[r, :] = dh if k == 0 else dh_acc[r, :] + dh

    def tok_load(i):
        return pltpu.make_async_copy(routed_ref.at[at(token_order[i])], routed_v.at[i % 2], tself_sem.at[i])

    def start_tok(i):
        token_owns[i].wait()
        wait_bytes(slots.at[0, pl.ds(0, rows - cap)], tpush_recv.at[i])
        tok_load(i).start()

    def add_tok(i):
        tok_load(i).wait()
        w = weight_block(at(token_order[i]))
        for j in range(rows // tile):
            r = pl.ds(j * tile, tile)
            gu = jnp.dot(routed_v[i % 2, r, :], w, preferred_element_type=F32)
            gu_acc[r, :] = gu if i == 0 else gu_acc[r, :] + gu

    def weight_block(o):
        r = pl.ds(pl.multiple_of(o * width, 128), width)
        return jnp.concatenate([wg_ref[r, :], wu_ref[r, :]], axis=1)

    def fill_bk(d, o, into):
        w = weight_block(o)
        for i in range(half // tile):
            lhs = dgu_ref[pl.ds(d * half + i * tile, tile), :]
            into[d, pl.ds(i * tile, tile), :] = lax.dot_general(
                lhs, w, NT_DIMS, preferred_element_type=F32
            ).astype(into.dtype)

    def rs_copy(k, d, p):
        size = half // RS_PIECES
        r = pl.ds(p * size, size)
        return remote(
            rs0.at[d, r] if k == 0 else rs.at[d, k - 1, r], rs.at[d, k, r],
            rs_send.at[d, k, p], rs_recv.at[d, k, p], expert=me, tensor=(right, left)[d],
        )

    push_tok(0)
    token_step(1)
    wait_bytes(cslots.at[pl.ds(0, rows - cap)], cpush_recv)
    own_cot.wait()
    cot_step(0)
    token_step(2)
    cot_step(1)
    for c in weight_loads:
        c.wait()
    add_cot(0)
    token_step(3)
    cot_step(2)
    add_cot(1)
    token_step(4)
    cot_step(3)
    start_tok(0)
    add_cot(2)
    start_tok(1)
    add_tok(0)
    cot_step(4)
    start_tok(2)
    add_cot(3)
    add_tok(1)
    start_tok(3)
    add_tok(2)
    cot_step(5)
    start_tok(4)
    add_cot(4)
    add_tok(3)
    start_tok(5)
    add_tok(4)
    cot_step(6)
    start_tok(6)
    add_cot(5)
    add_tok(5)
    add_tok(6)
    add_cot(6)
    lanes = lax.broadcasted_iota(jnp.int32, (n_tok, rows), 1).astype(F32)
    for k, target in enumerate(slot_targets(id_rows, id_cols, cap, 1)):
        pick[pl.ds(k * n_tok, n_tok), :] = jnp.where(lanes == target, 1.0, 0.0).astype(BF16)
    start_tok(7)
    add_tok(7)

    def gates(r):
        gate, up = gu_acc[r, :h], gu_acc[r, h:]
        sig = 1.0 / (1.0 + jnp.exp(-gate))
        return gate, up, sig, gate * sig

    for j in range(rows // tile):
        r = pl.ds(j * tile, tile)
        gate, up, sig, silu = gates(r)
        hid_ref[r, :] = (silu * up).astype(BF16)
    for i in range(nz):
        wait_bytes(slots.at[0, pl.ds(0, rows - cap)], tpush_send.at[i])

    split = 128 * ((width // 128 + 1) // 2)
    parts = ((0, split), (split, width - split))
    owns = {}

    def down(u, sides=(0, 1)):
        for d in sides:
            o = at((-1 - u, 1 + u)[d])
            first, count = parts[d]
            cols, here = pl.ds(pl.multiple_of(o * width + first, 128), count), pl.ds(first, count)

            def body(j, _):
                r = pl.ds(pl.multiple_of(j * tile, tile), tile)
                slots[o, r, here] = jnp.dot(hid_ref[r, :], wd_ref[:, cols], preferred_element_type=F32).astype(BF16)
                return 0

            lax.fori_loop(0, rows // tile, body, 0)

            def push(j, _):
                q = lax.rem(me + j, nx)
                remote(
                    slots.at[o, slab(q), here], ret.at[o, slab(me), here],
                    push_send.at[d, u], push_recv.at[d, u], expert=q, tensor=t,
                ).start()
                return 0

            lax.fori_loop(1, nx, push, 0)
            own = pltpu.make_async_copy(slots.at[o, slab(me), here], ret.at[o, slab(me), here], self_sem.at[d, u])
            own.start()
            owns[d, u] = own

    down(0, (0,))
    cot_step(7)
    down(0, (1,))
    add_cot(7)
    for j in range(rows // tile):
        r = pl.ds(j * tile, tile)
        gate, up, sig, silu = gates(r)
        d_hidden = dh_acc[r, :]
        dgu_ref[r, :h] = (d_hidden * up * sig * (1.0 + gate * (1.0 - sig))).astype(BF16)
        dgu_ref[r, h:] = (d_hidden * silu).astype(BF16)
        dots = jnp.sum(hid_ref[r, :].astype(F32) * d_hidden, axis=1, keepdims=True)
        dsrc[r, :] = jnp.broadcast_to(dots, (tile, dsrc.shape[1]))

    def push_dots(i, _):
        q = lax.rem(me + i, nx)
        remote(dsrc.at[slab(q)], dret.at[slab(me)], d_send, d_recv, expert=q, tensor=t).start()
        return 0

    for d in range(2):
        fill_bk(d, at((-1, 1)[d]), rs0)
        for p in range(RS_PIECES):
            go(rs_copy(0, d, p))
    down(1)
    lax.fori_loop(1, nx, push_dots, 0)
    dret[slab(me), :] = dsrc[slab(me), :]
    hid_t[...] = hid_ref[...].astype(F32).T.astype(BF16)
    dgu_t[...] = dgu_ref[...].astype(F32).T.astype(BF16)

    def load(o):
        return (
            pltpu.make_async_copy(routed_ref.at[o], routed_v.at[o % 2], load_sem.at[0, o % 2]),
            pltpu.make_async_copy(rcot_ref.at[o], rcot_v.at[o % 2], load_sem.at[1, o % 2]),
        )

    for c in load(0):
        c.start()

    def grads(o):
        for c in load(o):
            c.wait()
        if o + 1 < nz:
            for c in load(o + 1):
                c.start()
        s = o % 2
        r = pl.ds(o * width, width)
        gd_ref[:, r] = jnp.dot(hid_t[...], rcot_v[s], preferred_element_type=F32).astype(BF16)
        both = jnp.dot(dgu_t[...], routed_v[s], preferred_element_type=F32).T.astype(BF16)
        gg_ref[r, :] = both[:, :h]
        gu_ref[r, :] = both[:, h:]

    def rs2_copy(k, d, p):
        cols, size = pl.ds(*parts[d]), n_tok // RS_PIECES
        r = pl.ds(p * size, size)
        return remote(
            rs2_0.at[r, cols] if k == 0 else rs2.at[k - 1, r, cols], rs2.at[k, r, cols],
            rs2_send.at[d, k, p], rs2_recv.at[d, k, p], expert=me, tensor=(right, left)[d],
        )

    def rs2_step(u):
        for d in range(2):
            o, cols = at((-1 - u, 1 + u)[d]), pl.ds(*parts[d])
            owns[d, u].wait()
            wait_bytes(ret.at[0, pl.ds(0, rows - cap), cols], push_recv.at[d, u])
            chosen = jnp.dot(pick[...], ret[o, :, cols], preferred_element_type=F32)
            mix_v[:, cols] = w_col_ref[:, 0:1] * chosen[:n_tok] + w_col_ref[:, 1:2] * chosen[n_tok:]
        for p in range(RS_PIECES):
            r = pl.ds(p * (n_tok // RS_PIECES), n_tok // RS_PIECES)
            for d in range(2):
                cols = pl.ds(*parts[d])
                part = mix_v[r, cols]
                if u == 0:
                    rs2_0[r, cols] = part.astype(BF16)
                else:
                    rs2_copy(u - 1, d, p).wait_recv()
                    part = rs2[u - 1, r, cols].astype(F32) + part
                    if u < nz - 1:
                        rs2[u - 1, r, cols] = part.astype(BF16)
                    else:
                        mixed_ref[r, cols] = part.astype(BF16)
                if u < nz - 1:
                    go(rs2_copy(u, d, p))

    def route_part():
        wait_bytes(dret.at[pl.ds(0, rows - cap)], d_recv)
        j = lax.broadcasted_iota(jnp.int32, (rows, n_tok), 0).astype(F32)
        dpart[...] = jnp.zeros_like(dpart)
        for k, target in enumerate(row_targets):
            dpart[k : k + 1, :] = jnp.sum(jnp.where(j == target, dret[...], 0.0), axis=0, keepdims=True)

        def share(i, _):
            remote(dpart, dsum.at[t], z_send, z_recv, expert=me, tensor=lax.rem(t + i, nz)).start()
            return 0

        lax.fori_loop(1, nz, share, 0)
        dsum[t] = dpart[...]

    size = half // RS_PIECES
    for k in range(1, nz):
        for d in range(2):
            fill_bk(d, at((-1 - k, 1 + k)[d]), bk)
        if k + 1 < nz:
            down(k + 1)
        if k == 1:
            grads(0)
        for p in range(RS_PIECES):
            r = pl.ds(p * size, size)
            for d in range(2):
                rs_copy(k - 1, d, p).wait_recv()
                total = (rs[d, k - 1, r, :].astype(F32) + bk[d, r, :]).astype(BF16)
                if k < nz - 1:
                    rs[d, k - 1, r, :] = total
                    go(rs_copy(k, d, p))
                    continue
                islots[pl.ds(d * half + p * size, size), :] = total
                first, count = (d * half + p * size) // cap, size // cap

                def push_grad(i, _):
                    q = first + lax.rem(me + i, count)

                    @pl.when(q != me)
                    def _():
                        remote(islots.at[slab(q)], gret.at[slab(me)], g_send, g_recv, expert=q, tensor=t).start()

                    return 0

                lax.fori_loop(0, count, push_grad, 0)
        grads(k)
        if k == 4:
            route_part()
        if k >= RS2_LAG:
            rs2_step(k - RS2_LAG)
    gret[slab(me), :] = islots[slab(me), :]
    for u in range(nz - RS2_LAG, nz - 1):
        rs2_step(u)
    wait_bytes(gret.at[pl.ds(0, rows - cap)], g_recv)
    chosen = jnp.dot(pick[...], gret[...], preferred_element_type=F32)
    gtok_ref[...] = (w_col_ref[:, 0:1] * chosen[:n_tok] + w_col_ref[:, 1:2] * chosen[n_tok:]).astype(BF16)
    rs2_step(nz - 1)

    wait_bytes(dsum.at[pl.ds(0, nz - 1)], z_recv)
    total = dsum[0]
    for z in range(1, nz):
        total = total + dsum[z]
    groute_ref[...] = total[0:2, :] / w_row_ref[...]

    for c in started:
        c.wait_send()
    for d in range(2):
        for u in range(nz):
            wait_bytes(ret.at[0, pl.ds(0, rows - cap), pl.ds(*parts[d])], push_send.at[d, u])
    wait_bytes(islots.at[pl.ds(0, rows - cap)], g_send)
    wait_bytes(dsrc.at[pl.ds(0, rows - cap)], d_send)
    wait_bytes(dsum.at[pl.ds(0, nz - 1)], z_send)
    wait_bytes(cslots.at[pl.ds(0, rows - cap)], cpush_send)


def layer(nx, nz, cap, ids_t, weights_t, tokens, cotangent, wg, wu, wd):
    n_tok, width = tokens.shape
    h = wg.shape[1]
    rows = nx * cap
    dma = pltpu.SemaphoreType.DMA
    small = pltpu.VMEM((n_tok, width), BF16)
    tall = pltpu.VMEM((nz * width, h), BF16)
    buffer = jax.ShapeDtypeStruct((nz, rows, width), BF16)
    return pl.pallas_call(
        functools.partial(layer_kernel, nx, nz, cap),
        out_shape=(
            buffer, buffer, small, small, pltpu.VMEM((2, n_tok), F32), tall, tall,
            pltpu.VMEM((h, nz * width), BF16),
        ),
        in_specs=[VMEM] * 4 + [ANY] * 3,
        out_specs=(ANY, ANY, VMEM, VMEM, VMEM, VMEM, VMEM, VMEM),
        scratch_shapes=[
            pltpu.VMEM((nz * width, h), BF16),
            pltpu.VMEM((nz * width, h), BF16),
            pltpu.VMEM((h, nz * width), BF16),
            pltpu.VMEM((rows, n_tok), BF16),
            pltpu.VMEM((nz, n_tok, width), BF16),
            pltpu.VMEM((nz, rows, width), BF16),
            pltpu.VMEM((rows, width), BF16),
            pltpu.VMEM((rows, 2 * h), F32),
            pltpu.VMEM((rows, h), F32),
            pltpu.VMEM((rows, h), BF16),
            pltpu.VMEM((rows, 2 * h), BF16),
            pltpu.VMEM((n_tok, 2), F32),
            pltpu.VMEM((2 * n_tok, rows), BF16),
            pltpu.VMEM((h, rows), BF16),
            pltpu.VMEM((2 * h, rows), BF16),
            pltpu.VMEM((nz, rows, width), BF16),
            pltpu.VMEM((2, rows // 2, width), BF16),
            pltpu.VMEM((2, nz - 1, rows // 2, width), BF16),
            pltpu.VMEM((2, rows // 2, width), F32),
            pltpu.VMEM((rows, width), BF16),
            pltpu.VMEM((rows, width), BF16),
            pltpu.VMEM((n_tok, width), F32),
            pltpu.VMEM((n_tok, width), BF16),
            pltpu.VMEM((nz - 1, n_tok, width), BF16),
            pltpu.VMEM((rows, 128), F32),
            pltpu.VMEM((rows, 128), F32),
            pltpu.VMEM((8, n_tok), F32),
            pltpu.VMEM((nz, 8, n_tok), F32),
            pltpu.VMEM((2, rows, width), BF16),
            pltpu.VMEM((2, rows, width), BF16),
            dma((2, nz // 2, PIECES)), dma((2, nz // 2, PIECES)), dma((nz,)), dma((nz,)), dma((nz,)), dma, dma, dma,
            dma((2, nz - 1, PIECES)), dma((2, nz - 1, PIECES)), dma((2, 2, PIECES)), dma((3,)),
            dma((2, nz)), dma((2, nz)), dma((2, nz)),
            dma((2, nz - 1, RS_PIECES)), dma((2, nz - 1, RS_PIECES)),
            dma, dma, dma((2, nz - 1, RS_PIECES)), dma((2, nz - 1, RS_PIECES)),
            dma, dma, dma, dma, dma((2, 2)),
        ],
        compiler_params=pltpu.CompilerParams(
            collective_id=0, has_side_effects=True, vmem_limit_bytes=52 * 1024 * 1024
        ),
        name="layer",
    )(ids_t, weights_t, tokens, cotangent, wg, wu, wd)


CHUNKS = 4


def finish_kernel(*refs):
    n = 6
    ins, outs, put = refs[:n], refs[n : 2 * n], refs[2 * n]
    moves = []
    for src, dst in zip(ins, outs):
        axis = 0 if src.shape[0] >= src.shape[1] else 1
        count = CHUNKS if max(src.shape) >= 1024 * CHUNKS else 1
        size = src.shape[axis] // count
        for c in range(count):
            where = (pl.ds(c * size, size), slice(None)) if axis == 0 else (slice(None), pl.ds(c * size, size))
            moves.append(pltpu.make_async_copy(src.at[where], dst.at[where], put.at[len(moves)]))
    for move in moves:
        move.start()
    for move in moves:
        move.wait()


def finish(*arrays):
    n = len(arrays)
    shapes = tuple(jax.ShapeDtypeStruct(a.shape, a.dtype) for a in arrays)
    return pl.pallas_call(
        finish_kernel,
        out_shape=shapes,
        in_specs=[VMEM] * n,
        out_specs=(ANY,) * n,
        scratch_shapes=[pltpu.SemaphoreType.DMA((n * CHUNKS,))],
        compiler_params=pltpu.CompilerParams(vmem_limit_bytes=16 * 1024 * 1024),
        name="finish",
    )(*arrays)


def local(tokens, ids, weights, cotangent, w_gate, w_up, w_down):
    nx, nz = lax.axis_size("expert"), lax.axis_size("tensor")
    cap = 4 * tokens.shape[0] // nx
    results = layer(nx, nz, cap, ids.T, weights.T, tokens, cotangent, w_gate[0], w_up[0], w_down[0])
    mixed, grad_tokens, grad_route, grad_gate, grad_up, grad_down = finish(*results[2:])
    return (mixed, grad_tokens, grad_route.T, grad_gate[None], grad_up[None], grad_down[None])


def solution(mesh):
    placed = (
        P("expert", "tensor"),
        P("expert", None),
        P("expert", None),
        P("expert", "tensor"),
        P("expert", None, "tensor"),
        P("expert", None, "tensor"),
        P("expert", "tensor", None),
    )
    return jax.shard_map(
        local,
        mesh=mesh,
        in_specs=placed,
        out_specs=(
            P("expert", "tensor"),
            P("expert", "tensor"),
            P("expert", None),
            P("expert", None, "tensor"),
            P("expert", None, "tensor"),
            P("expert", "tensor", None),
        ),
        check_vma=False,
    )
```
